32 devices in a mesh: clips: 2 (over x), segment: 2 (over core), rows: 8 (over z, y).
Axes of the slice: x: 2, y: 2, z: 4, core: 2. Of those that a mesh axis runs over, the one named last changes fastest.
Arguments:
- latent: float32 [4, 48, 512], P('clips', 'rows', 'segment'), parts along dimension 0, may hold values from -6 to 6
- stale: bfloat16 [2, 4, 48, 128, 320], P('segment', 'clips', 'rows'), parts along dimension 1, may hold values from -6 to 6
- timesteps: int32 [4], P('clips'), parts along dimension 0, may hold values from 0 to 999
- w_in: bfloat16 [4, 320], replicated, may hold values from -3 to 3
- w_enc: bfloat16 [3, 3, 320, 320], replicated, may hold values from -0.109375 to 0.109375
- w_down: bfloat16 [3, 3, 320, 640], replicated, may hold values from -0.109375 to 0.109375
- w_tmid: bfloat16 [3, 640, 640], replicated, may hold values from -0.125 to 0.125
- w_up: bfloat16 [640, 320], replicated, may hold values from -0.25 to 0.25
- w_skip: bfloat16 [640, 320], replicated, may hold values from -0.25 to 0.25
- w_dec: bfloat16 [3, 3, 320, 320], replicated, may hold values from -0.109375 to 0.109375
- w_out: bfloat16 [3, 3, 320, 4], replicated, may hold values from -0.109375 to 0.109375
- w_time: bfloat16 [320, 1280], replicated, may hold values from -0.3125 to 0.3125
Outputs:
- next_latent: float32 [4, 48, 512], P('clips', 'rows', 'segment'), parts along dimension 0
- features: bfloat16 [2, 4, 48, 128, 320], P('segment', 'clips', 'rows'), parts along dimension 1
The draws below stay inside these ranges and needn't reach their ends.
There are 2 independent parts, one for each index of `clips`. The reference program is written for one: setup_inputs(seed, part) draws one part's arguments, and reference() takes and returns one part's arrays. A program takes and returns all parts, laid end to end along the dimension named above; an argument that names none is the same for every part. Nothing has to cross between parts.
Inputs may be any that keep to these rules, and one draw needn't show every extreme that they name: `timesteps`: one diffusion timestep index a step.
All inputs are finite; a program needn't handle non-finite values.
Results may differ from the reference program's by a relative error of at most 0.006.
Values may be sent and summed in bfloat16 or wider, within the bound.
No kernel may reach another device: no remote copies, remote signals or barrier semaphores. Data moves between devices by JAX's collectives and lax.ppermute only.
A program may use at most 128 MiB of HBM per device.

```python
import math
import jax
import jax.numpy as jnp
from jax import lax

C_ENC = 320
C_MID = 640
LAT = 4
WIDTH_LAT = 128
FRAMES = 2
STEPS = 2
HEIGHT = 48


def shard_levels(key, extent, cuts, low, largest):
    level, own = 1.0, jax.random.fold_in(key, 6)
    for dim, blocks in cuts:
        heights = jnp.exp(jax.random.uniform(jax.random.fold_in(own, dim), (blocks,), jnp.float32, low / len(cuts), largest / len(cuts)))
        level = level * jnp.repeat(heights, extent[dim] // blocks).reshape([-1 if axis == dim else 1 for axis in range(len(extent))])
    return level


def gaussian(stream_key, dims, scale, reach, cuts=(), kind=jnp.bfloat16):
    result = scale * jax.random.normal(stream_key, dims, jnp.float32)
    if cuts:
        result = result * shard_levels(stream_key, dims, cuts, -0.22, 0.18)
    return jnp.clip(result, -reach, reach).astype(kind)


def setup_inputs(seed: int = 0, part: int = 0) -> dict:
    keys = jax.random.split(jax.random.key(seed), 13)
    part_keys = jax.random.split(jax.random.fold_in(keys[12], part), 13)
    latent = gaussian(part_keys[0], (FRAMES, HEIGHT, WIDTH_LAT * LAT), 1.0, 6.0, ((1, 8), (2, 2)), jnp.float32)
    stale = gaussian(part_keys[1], (2, FRAMES, HEIGHT, WIDTH_LAT, C_ENC), 1.0, 6.0, ((0, 2), (2, 8)))
    timesteps = jax.random.randint(part_keys[2], (STEPS,), 0, 1000).astype(jnp.int32)
    w_in = gaussian(keys[3], (LAT, C_ENC), LAT ** -0.5, 3.0)
    w_enc = gaussian(keys[4], (3, 3, C_ENC, C_ENC), (9 * C_ENC) ** -0.5, 0.109375)
    w_down = gaussian(keys[5], (3, 3, C_ENC, C_MID), (9 * C_ENC) ** -0.5, 0.109375)
    w_tmid = gaussian(keys[6], (3, C_MID, C_MID), (3 * C_MID) ** -0.5, 0.125)
    w_up = gaussian(keys[7], (C_MID, C_ENC), C_MID ** -0.5, 0.25)
    w_skip = gaussian(keys[8], (2 * C_ENC, C_ENC), (2 * C_ENC) ** -0.5, 0.25)
    w_dec = gaussian(keys[9], (3, 3, C_ENC, C_ENC), (9 * C_ENC) ** -0.5, 0.109375)
    w_out = gaussian(keys[10], (3, 3, C_ENC, LAT), (9 * C_ENC) ** -0.5, 0.109375)
    w_time = gaussian(keys[11], (C_ENC, 2 * C_ENC + C_MID), C_ENC ** -0.5, 0.3125)
    return {"latent": latent, "stale": stale, "timesteps": timesteps, "w_in": w_in, "w_enc": w_enc, "w_down": w_down, "w_tmid": w_tmid, "w_up": w_up, "w_skip": w_skip, "w_dec": w_dec, "w_out": w_out, "w_time": w_time}


EPSILON = 1e-06

def einsum32(form, left, right):
    return jnp.einsum(form, left.astype(jnp.float32), right.astype(jnp.float32))

def normed(values):
    scale = lax.rsqrt(lax.optimization_barrier(jnp.mean(values * values, axis=-1, keepdims=True)) + EPSILON)
    return jax.nn.silu(values * scale)

def pad_rows(values):
    return jnp.pad(values, ((0, 0), (1, 1), (0, 0), (0, 0)))

def conv_rows(extended, weight, count):
    padded = jnp.pad(extended, ((0, 0), (0, 0), (1, 1), (0, 0)))
    columns = extended.shape[2]
    total = jnp.zeros((extended.shape[0], count, columns, weight.shape[3]), jnp.float32)
    for row_off in range(3):
        for col_off in range(3):
            window = padded[:, row_off:row_off + count, col_off:col_off + columns, :]
            total = total + einsum32('fhwc,co->fhwo', window, weight[row_off, col_off])
    return total

def conv_down(extended, weight, count):
    padded = jnp.pad(extended, ((0, 0), (0, 0), (1, 1), (0, 0)))
    columns = extended.shape[2] // 2
    total = jnp.zeros((extended.shape[0], count, columns, weight.shape[3]), jnp.float32)
    for row_off in range(3):
        for col_off in range(3):
            window = padded[:, row_off:row_off + 2 * count:2, col_off:col_off + 2 * columns:2, :]
            total = total + einsum32('fhwc,co->fhwo', window, weight[row_off, col_off])
    return total

def temporal(values, weight):
    frames = values.shape[0]
    padded = jnp.pad(values, ((1, 1), (0, 0), (0, 0), (0, 0)))
    total = jnp.zeros(values.shape[:3] + (weight.shape[2],), jnp.float32)
    for offset in range(3):
        total = total + einsum32('fhwc,co->fhwo', padded[offset:offset + frames], weight[offset])
    return total

def time_bias(step_time, w_time):
    half = w_time.shape[0] // 2
    freqs = jnp.exp(-math.log(10000.0) * jnp.arange(half).astype(jnp.float32) / half)
    angles = step_time.astype(jnp.float32) * freqs
    embedded = jnp.concatenate([jnp.sin(angles), jnp.cos(angles)])
    gated = jax.nn.silu(embedded).astype(jnp.bfloat16)
    return jnp.dot(gated[None, :], w_time, preferred_element_type=jnp.float32)[0]

def reference(latent, stale, timesteps, w_in, w_enc, w_down, w_tmid, w_up, w_skip, w_dec, w_out, w_time):
    chans = w_enc.shape[3]
    mid_chans = w_down.shape[3]
    current = latent
    enc_map = stale[0]
    mid_map = stale[1]
    for step in range(STEPS):
        biases = time_bias(timesteps[step], w_time)
        bias_enc = biases[:chans]
        bias_mid = biases[chans:chans + mid_chans]
        bias_dec = biases[chans + mid_chans:]
        inputs = current.reshape(FRAMES, HEIGHT, WIDTH_LAT, LAT).astype(jnp.bfloat16)
        lifted = einsum32('fhwc,co->fhwo', inputs, w_in)
        activated = normed(lifted).astype(jnp.bfloat16)
        fresh_enc = (lifted + conv_rows(pad_rows(activated), w_enc, HEIGHT) + bias_enc).astype(jnp.bfloat16)
        gated_enc = normed(enc_map.astype(jnp.float32)).astype(jnp.bfloat16)
        lowered = conv_down(pad_rows(gated_enc), w_down, HEIGHT // 2) + bias_mid
        mixed_time = lowered + temporal(normed(lowered).astype(jnp.bfloat16), w_tmid)
        raised = einsum32('fhwc,co->fhwo', mixed_time.astype(jnp.bfloat16), w_up).astype(jnp.bfloat16)
        fresh_mid = jnp.repeat(jnp.repeat(raised, 2, axis=1), 2, axis=2)
        joined = jnp.concatenate([mid_map, enc_map], axis=-1)
        mixed = einsum32('fhwc,co->fhwo', joined, w_skip)
        gated = normed(mixed).astype(jnp.bfloat16)
        decoded = mixed + conv_rows(pad_rows(gated), w_dec, HEIGHT) + bias_dec
        outlet = normed(decoded).astype(jnp.bfloat16)
        noise = conv_rows(pad_rows(outlet), w_out, HEIGHT)
        coefficient = (timesteps[step].astype(jnp.float32) + 1.0) / 1000.0
        current = current - coefficient * noise.reshape(FRAMES, HEIGHT, WIDTH_LAT * LAT)
        enc_map = fresh_enc
        mid_map = fresh_mid
    return (current, jnp.stack([enc_map, mid_map]))
```

```python
import functools
import math

import jax
import jax.numpy as jnp
from jax import lax
from jax.experimental import pallas as pl
from jax.experimental.pallas import tpu as pltpu
from jax.sharding import PartitionSpec as P

EPSILON = 1e-06
LANES = 128
LANE_CH = 8
F32 = jnp.float32
BF16 = jnp.bfloat16

VMEM = pl.BlockSpec(memory_space=pltpu.VMEM)
SMEM = pl.BlockSpec(memory_space=pltpu.SMEM)


def act(values):
    scale = lax.rsqrt(jnp.mean(values * values, axis=-1, keepdims=True) + EPSILON)
    half = values * (0.5 * scale)
    return half + half * jnp.tanh(half)


def dot(left, right):
    return jnp.dot(left, right, preferred_element_type=F32)


def shifted(values, by):
    count = values.shape[0]
    column = lax.broadcasted_iota(jnp.int32, values.shape, 0)
    edge = 0 if by == 1 else count - 1
    return jnp.where(column == edge, 0.0, pltpu.roll(values, by % count, 0))


def lane_shifted(values, by):
    count = values.shape[1]
    column = lax.broadcasted_iota(jnp.int32, values.shape, 1)
    edge = 0 if by == 1 else count - 1
    return jnp.where(column == edge, 0.0, pltpu.roll(values, by % count, 1))


def call(kernel, outs, in_specs, scratch=(), name=None):
    return pl.pallas_call(
        kernel,
        out_shape=[jax.ShapeDtypeStruct(s, d) for s, d in outs],
        in_specs=in_specs,
        out_specs=[VMEM] * len(outs),
        scratch_shapes=[pltpu.VMEM(s, d) for s, d in scratch],
        name=name,
    )


def prep_kernel(enc_ref, dec_ref, enc_out, dec_out):
    chans = enc_ref.shape[3]
    for src, dst in ((enc_ref, enc_out), (dec_ref, dec_out)):
        for dy in range(3):
            for dx in range(3):
                dst[dy * chans : (dy + 1) * chans, dx * chans : (dx + 1) * chans] = src[dy, dx]


def spread_rows(acat_ref, row, value, cols, chans):
    for dy in range(3):
        start = pl.multiple_of((row - dy + 2) * cols, cols)
        acat_ref[pl.ds(start, cols), dy * chans : (dy + 1) * chans] = value


def conv_sum(acc_ref, row, cols, chans):
    taps = acc_ref.at[pl.ds(pl.multiple_of(row * cols, cols), cols), :]
    return (
        taps[:, chans : 2 * chans]
        + shifted(taps[:, :chans], 1)
        + shifted(taps[:, 2 * chans :], -1)
    )


def conv_product(acat_ref, wcat_ref, acc_ref, rows, cols):
    acc_ref[...] = dot(acat_ref[2 * cols : (2 + rows) * cols, :], wcat_ref[...])


def encode_rows(read_row, w_in_ref, wcat_ref, bias_ref, edges, out_ref, lift_ref, acat_ref, acc_ref):
    count, cols, chans = out_ref.shape
    border = edges[2]

    def front(row, carry):
        lifted = lax.dot_general(
            read_row(row), w_in_ref[...], (((0,), (0,)), ((), ())), preferred_element_type=F32
        )
        lift_ref[row] = lifted
        spread_rows(acat_ref, row, act(lifted).astype(BF16), cols, chans)
        return carry

    lax.fori_loop(0, count + 2, front, 0)
    conv_product(acat_ref, wcat_ref, acc_ref, count, cols)

    def back(row, carry):
        total = lift_ref[row + 1] + conv_sum(acc_ref, row, cols, chans) + bias_ref[...]
        outside = ((row < border) & (edges[0] == 1)) | ((row >= count - border) & (edges[1] == 1))
        out_ref[row] = jnp.where(outside, 0.0, total).astype(BF16)
        return carry

    lax.fori_loop(0, count, back, 0)


def enc_first_kernel(edge_ref, x_ref, w_in_ref, wcat_ref, bias_ref, out_ref, lift_ref, acat_ref, acc_ref):
    edges = (edge_ref[0], edge_ref[1], 2)
    encode_rows(
        lambda row: x_ref[row], w_in_ref, wcat_ref, bias_ref, edges, out_ref, lift_ref, acat_ref, acc_ref
    )


def enc_last_kernel(
    edge_ref, base_ref, near_ref, up_ref, down_ref, w_in_ref, wcat_ref, bias_ref,
    out_ref, x_ref, ext_ref, lift_ref, acat_ref, acc_ref,
):
    rows = base_ref.shape[0]
    lanes = base_ref.shape[2]
    low_cols = up_ref.shape[0] - 4 * LANE_CH

    def received(ref):
        span = 2 * LANE_CH
        high = ref[low_cols : low_cols + span, :lanes].astype(F32)
        low = ref[low_cols + span : low_cols + 2 * span, :lanes].astype(F32)
        both = high + low
        return both[:LANE_CH], both[LANE_CH:]

    from_up, base_up = received(up_ref)
    from_down, base_down = received(down_ref)
    x_ref[...] = base_ref[...]
    x_ref[0] = x_ref[0] - from_up
    x_ref[rows - 1] = x_ref[rows - 1] - from_down
    ext_ref[0] = jnp.where(edge_ref[0] == 1, 0.0, base_up - near_ref[0]).astype(BF16)
    ext_ref[rows + 1] = jnp.where(edge_ref[1] == 1, 0.0, base_down - near_ref[1]).astype(BF16)
    ext_ref[1 : rows + 1] = x_ref[...].astype(BF16)
    encode_rows(
        lambda row: ext_ref[row], w_in_ref, wcat_ref, bias_ref, (edge_ref[0], edge_ref[1], 0),
        out_ref, lift_ref, acat_ref, acc_ref,
    )


def down_kernel(enc_ref, w_ref, bias_ref, low_ref, q_ref, gate_ref, acat_ref, *, first):
    cols, chans = enc_ref.shape[1:]
    half = cols // 2
    low_rows = low_ref.shape[0] // half
    spare = jnp.zeros((half, chans), F32)
    column = lax.broadcasted_iota(jnp.int32, spare.shape, 0)
    for row in range(2 * low_rows + 1):
        gate = act(enc_ref[first + row].astype(F32))
        for start in range(0, chans, LANES):
            wide = min(LANES, chans - start)
            gate_ref[row, start // LANES, :, :wide] = gate[:, start : start + wide]
        even, odd = (
            jnp.concatenate(
                [
                    gate_ref[row, start // LANES, pl.ds(offset, half, stride=2), :][:, : chans - start]
                    for start in range(0, chans, LANES)
                ],
                axis=1,
            )
            for offset in range(2)
        )
        before = jnp.where(column == 0, 0.0, pltpu.roll(odd, 1, 0))
        for dy in range(3):
            if (row - dy) % 2 or not 0 <= (row - dy) // 2 < low_rows:
                continue
            low = (row - dy) // 2
            for dx, part in enumerate((before, even, odd)):
                lane = (3 * dy + dx) * chans
                acat_ref[low * half : (low + 1) * half, lane : lane + chans] = part.astype(BF16)
    low_ref[...] = dot(acat_ref[...], w_ref[...]) + bias_ref[...]
    q_ref[...] = act(low_ref[...]).astype(BF16)


def raise_rows(pick_ref, low_ref, q_ref, other_ref, w_tmid_ref, w_up_ref):
    mixed = low_ref[...] + dot(q_ref[...], w_tmid_ref[1]) + dot(other_ref[...], w_tmid_ref[pick_ref[0]])
    return dot(mixed.astype(BF16), w_up_ref[...]).astype(BF16)


def mid_first_kernel(
    pick_ref, low_ref, q_ref, other_ref, w_tmid_ref, w_up_ref, base_ref, near_ref,
    raised_ref, up_ref, down_ref,
):
    raised_ref[...] = raise_rows(pick_ref, low_ref, q_ref, other_ref, w_tmid_ref, w_up_ref)
    rows, _, lanes = base_ref.shape
    half = up_ref.shape[0] - 4 * LANE_CH
    total = raised_ref.shape[0]
    span = 2 * LANE_CH
    for ref, start, edge, index in ((up_ref, 0, 0, 0), (down_ref, total - half, rows - 1, 1)):
        ref[:half, :] = raised_ref[start : start + half, :]
        sent = jnp.concatenate([near_ref[index], base_ref[edge]], axis=0)
        high = sent.astype(BF16)
        ref[half : half + span, :lanes] = high
        ref[half + span :, :lanes] = (sent - high.astype(F32)).astype(BF16)


def doubling(cols, half):
    row = lax.broadcasted_iota(jnp.int32, (cols, half), 0)
    col = lax.broadcasted_iota(jnp.int32, (cols, half), 1)
    return jnp.where((row == 2 * col) | (row == 2 * col + 1), 1.0, 0.0).astype(BF16)


def mid_last_kernel(
    pick_ref, low_ref, q_ref, other_ref, w_tmid_ref, w_up_ref, out_ref, raised_ref
):
    raised_ref[...] = raise_rows(pick_ref, low_ref, q_ref, other_ref, w_tmid_ref, w_up_ref)
    rows, cols, _ = out_ref.shape
    half = cols // 2
    twice = doubling(cols, half)
    for low in range(rows // 2):
        wide = dot(twice, raised_ref[low * half : (low + 1) * half, :]).astype(BF16)
        out_ref[2 * low] = wide
        out_ref[2 * low + 1] = wide


def decode_rows(count, cols, read_mixed, wcat_ref, bias_ref, edges, w_out_ref, mixed_ref, acat_ref, acc_ref, out_rows_ref):
    chans = bias_ref.shape[1]

    def front(row, carry):
        mixed = read_mixed(row)
        mixed_ref[row] = mixed
        spread_rows(acat_ref, row, act(mixed).astype(BF16), cols, chans)
        return carry

    lax.fori_loop(0, count + 2, front, 0)
    conv_product(acat_ref, wcat_ref, acc_ref, count, cols)

    def back(row, carry):
        total = mixed_ref[row + 1] + conv_sum(acc_ref, row, cols, chans) + bias_ref[...]
        value = act(total)
        if edges is not None:
            outside = ((row == 0) & (edges[0] == 1)) | ((row == count - 1) & (edges[1] == 1))
            value = jnp.where(outside, 0.0, value)
        start = pl.multiple_of(row * cols, cols)
        out_rows_ref[pl.ds(start, cols), :] = value.astype(BF16)
        return carry

    lax.fori_loop(0, count, back, 0)
    taps = lax.dot_general(
        w_out_ref[...], out_rows_ref[...], (((1,), (1,)), ((), ())), preferred_element_type=F32
    )
    span = 3 * LANE_CH
    parts = []
    for row in range(count):
        tap = taps[:, row * cols : (row + 1) * cols]
        parts.append(
            lane_shifted(tap[:span], 1) + tap[span : 2 * span] + lane_shifted(tap[2 * span :], -1)
        )
    return parts


def tap_sum(parts, row):
    total = None
    for dy in range(3):
        source = row + dy - 1
        if 0 <= source < len(parts):
            piece = parts[source][dy * LANE_CH : (dy + 1) * LANE_CH]
            total = piece if total is None else total + piece
    return total


def dec_first_kernel(
    coef_ref, enc_ref, mid_ref, x_ref, w_skip_ref, wcat_ref, bias_ref, w_out_ref,
    base_ref, near_ref, mixed_ref, acat_ref, acc_ref, out_rows_ref,
):
    rows = base_ref.shape[0]
    cols, chans = enc_ref.shape[1:]

    def read_mixed(row):
        return dot(mid_ref[row], w_skip_ref[:chans, :]) + dot(enc_ref[row], w_skip_ref[chans:, :])

    parts = decode_rows(
        rows, cols, read_mixed, wcat_ref, bias_ref, None, w_out_ref, mixed_ref, acat_ref, acc_ref, out_rows_ref
    )
    coef = coef_ref[0]
    halo = (x_ref.shape[0] - rows) // 2
    near_ref[0] = coef * tap_sum(parts, -1)
    near_ref[1] = coef * tap_sum(parts, rows)
    for row in range(rows):
        base_ref[row] = x_ref[halo + row] - coef * tap_sum(parts, row)


def dec_last_kernel(
    edge_ref, coef_ref, enc_ref, mid_ref, up_ref, down_ref, x_ref, w_skip_ref, wcat_ref, bias_ref, w_out_ref,
    next_ref, joined_ref, mixed_ref, acat_ref, acc_ref, out_rows_ref,
):
    rows = x_ref.shape[0]
    cols, chans = enc_ref.shape[1:]
    half = cols // 2
    inner = mid_ref.shape[0] // half
    twice = doubling(cols, half)
    for low in range(inner + 2):
        if low == 0:
            piece = up_ref[:half, :]
        elif low == inner + 1:
            piece = down_ref[:half, :]
        else:
            piece = mid_ref[(low - 1) * half : low * half, :]
        joined_ref[low] = dot(twice, piece).astype(BF16)

    def read_mixed(row):
        return dot(joined_ref[row // 2], w_skip_ref[:chans, :]) + dot(enc_ref[row], w_skip_ref[chans:, :])

    parts = decode_rows(
        rows + 2, cols, read_mixed, wcat_ref, bias_ref, (edge_ref[0], edge_ref[1]), w_out_ref,
        mixed_ref, acat_ref, acc_ref, out_rows_ref,
    )
    coef = coef_ref[1]
    for row in range(rows):
        next_ref[row] = x_ref[row] - coef * tap_sum(parts, row + 1)


def time_biases(timesteps, w_time):
    half = w_time.shape[0] // 2
    freqs = jnp.exp(-math.log(10000.0) * jnp.arange(half).astype(F32) / half)
    angles = timesteps.astype(F32)[:, None] * freqs[None, :]
    embedded = jnp.concatenate([jnp.sin(angles), jnp.cos(angles)], axis=1)
    gated = jax.nn.silu(embedded).astype(BF16)
    return jnp.dot(gated, w_time, preferred_element_type=F32)


def body(latent, stale, timesteps, w_in, w_enc, w_down, w_tmid, w_up, w_skip, w_dec, w_out, w_time):
    segment = lax.axis_index("segment")
    first = segment == 0
    size = lax.axis_size("rows")
    place = lax.axis_index("rows")
    state = stale[0]
    frames, rows, cols, chans = state.shape
    mid = w_down.shape[3]
    lat = w_in.shape[0]
    half = cols // 2
    low = (rows // 2) * half
    assert frames == 2 and lax.axis_size("segment") == 2

    up_pairs = [(i + 1, i) for i in range(size - 1)]
    down_pairs = [(i, i + 1) for i in range(size - 1)]

    def swap(value):
        return lax.ppermute(value, "segment", [(0, 1), (1, 0)])

    def from_above(value):
        return lax.ppermute(value, "rows", down_pairs)

    def from_below(value):
        return lax.ppermute(value, "rows", up_pairs)

    def mine(value):
        return lax.dynamic_index_in_dim(value, segment, 0, keepdims=False)

    def theirs(value):
        return lax.dynamic_index_in_dim(value, 1 - segment, 0, keepdims=False)

    halo = 3
    edge = latent.astype(BF16)
    x_up = from_above(edge[:, rows - halo :])
    x_down = from_below(edge[:, :halo])
    x_raw = jnp.concatenate([x_up.astype(F32), latent, x_down.astype(F32)], axis=1)
    x_mine, x_other = mine(x_raw), swap(theirs(x_raw))
    x_full = jnp.where(
        first,
        jnp.concatenate([x_mine, x_other], axis=1),
        jnp.concatenate([x_other, x_mine], axis=1),
    )
    x_t = x_full.reshape(rows + 2 * halo, cols, lat).transpose(0, 2, 1)
    x_t = jnp.pad(x_t, ((0, 0), (0, LANE_CH - lat), (0, 0)))

    s_up = from_above(state[:, rows - 1 :])
    s_down = from_below(state[:, :1])
    s_raw = jnp.concatenate([s_up, state, s_down], axis=1)
    s_mine, s_other = mine(s_raw), swap(theirs(s_raw))
    enc0 = jnp.where(first, s_mine, s_other)
    mid0 = jnp.where(first, s_other, s_mine)

    biases = time_biases(timesteps, w_time)
    b_enc = biases[:, :chans]
    b_mid = biases[:, chans : chans + mid]
    b_dec = biases[:, chans + mid :]
    coefs = (timesteps.astype(F32) + 1.0) / 1000.0
    edges = jnp.stack([place == 0, place == size - 1]).astype(jnp.int32)
    pick = (2 - 2 * segment).astype(jnp.int32)[None]

    w_in8 = jnp.pad(w_in, ((0, LANE_CH - lat), (0, 0)))
    w_taps = jnp.pad(w_out.transpose(1, 0, 3, 2), ((0, 0), (0, 0), (0, LANE_CH - lat), (0, 0)))
    w_taps = w_taps.reshape(9 * LANE_CH, chans)
    w_down2 = w_down.reshape(9 * chans, mid)

    enc_cat, dec_cat = call(
        prep_kernel, [((3 * chans, 3 * chans), BF16)] * 2, [VMEM] * 2, name="prep"
    )(w_enc, w_dec)

    def enc_scratch(count):
        return [
            ((count + 2, cols, chans), F32),
            (((count + 4) * cols, 3 * chans), BF16),
            ((count * cols, 3 * chans), F32),
        ]

    def dec_scratch(count):
        return enc_scratch(count) + [((count * cols, chans), BF16)]

    ext = rows + 4
    (enc1,) = call(
        enc_first_kernel, [((ext, cols, chans), BF16)], [SMEM] + [VMEM] * 4, enc_scratch(ext), "enc_first"
    )(edges, x_t.astype(BF16), w_in8, enc_cat, b_enc[0:1])

    down_outs = [((low, mid), F32), ((low, mid), BF16)]
    down_scratch = [((rows + 1, -(-chans // LANES), cols, LANES), F32), ((low, 9 * chans), BF16)]
    low0, q0 = call(
        functools.partial(down_kernel, first=0), down_outs, [VMEM] * 3, down_scratch, "down_first"
    )(enc0, w_down2, b_mid[0:1])
    q0_other = swap(q0)

    base, near = call(
        dec_first_kernel,
        [((rows, LANE_CH, cols), F32), ((2, LANE_CH, cols), F32)],
        [SMEM] + [VMEM] * 7,
        dec_scratch(rows),
        "dec_first",
    )(coefs, enc0, mid0, x_t, w_skip, dec_cat, b_dec[0:1], w_taps)

    bundle = (half + 4 * LANE_CH, chans)
    mid1, to_up, to_down = call(
        mid_first_kernel, [((low, chans), BF16), (bundle, BF16), (bundle, BF16)], [SMEM] + [VMEM] * 7, (), "mid_first"
    )(pick, low0, q0, q0_other, w_tmid, w_up, base, near)
    got_up = from_above(to_down)
    got_down = from_below(to_up)

    low1, q1 = call(
        functools.partial(down_kernel, first=1), down_outs, [VMEM] * 3, down_scratch, "down_last"
    )(enc1, w_down2, b_mid[1:2])
    q1_other = swap(q1)

    enc2, x1 = call(
        enc_last_kernel,
        [((rows, cols, chans), BF16), ((rows, LANE_CH, cols), F32)],
        [SMEM] + [VMEM] * 7,
        [((rows + 2, LANE_CH, cols), BF16)] + enc_scratch(rows),
        "enc_last",
    )(edges, base, near, got_up, got_down, w_in8, enc_cat, b_enc[1:2])

    (mid2,) = call(
        mid_last_kernel, [((rows, cols, chans), BF16)], [SMEM] + [VMEM] * 5, [((low, chans), BF16)], "mid_last"
    )(pick, low1, q1, q1_other, w_tmid, w_up)

    feat_other = swap(jnp.where(first, mid2, enc2))

    (x2,) = call(
        dec_last_kernel,
        [((rows, LANE_CH, cols), F32)],
        [SMEM] * 2 + [VMEM] * 9,
        [((rows // 2 + 2, cols, chans), BF16)] + dec_scratch(rows + 2),
        "dec_last",
    )(edges, coefs, enc1, mid1, got_up, got_down, x1, w_skip, dec_cat, b_dec[1:2], w_taps)

    flat = x2[:, :lat].transpose(0, 2, 1).reshape(rows, cols * lat)
    halves = jnp.stack([flat[:, : cols * lat // 2], flat[:, cols * lat // 2 :]])
    x_keep, x_got = mine(halves), swap(theirs(halves))
    result = jnp.where(first, jnp.stack([x_keep, x_got]), jnp.stack([x_got, x_keep]))
    features = jnp.where(first, jnp.stack([enc2, feat_other]), jnp.stack([feat_other, mid2]))
    return (result, features[None])


def solution(mesh):
    placed = (
        P("clips", "rows", "segment"),
        P("segment", "clips", "rows", None, None),
        P("clips"),
    ) + (P(),) * 9
    return jax.shard_map(
        body,
        mesh=mesh,
        in_specs=placed,
        out_specs=(P("clips", "rows", "segment"), P("segment", "clips", "rows", None, None)),
        check_vma=False,
    )
```

```python
import functools
import math

import jax
import jax.numpy as jnp
from jax import lax
from jax.experimental import pallas as pl
from jax.experimental.pallas import tpu as pltpu
from jax.sharding import PartitionSpec as P

EPSILON = 1e-06
LAT8 = 8
TILE = 16
F32 = jnp.float32
BF16 = jnp.bfloat16

VMEM = pl.BlockSpec(memory_space=pltpu.VMEM)
SMEM = pl.BlockSpec(memory_space=pltpu.SMEM)
ANY = pl.BlockSpec(memory_space=pl.ANY)


def act(values):
    scale = lax.rsqrt(jnp.mean(values * values, axis=0, keepdims=True) + EPSILON)
    half = values * (0.5 * scale)
    return half + half * jnp.tanh(half)


def dot(left, right):
    return jnp.dot(left, right, preferred_element_type=F32)


def shifted(values, by):
    count = values.shape[1]
    column = lax.broadcasted_iota(jnp.int32, values.shape, 1)
    edge = 0 if by == 1 else count - 1
    return jnp.where(column == edge, 0.0, pltpu.roll(values, by % count, 1))


def call(kernel, outs, in_specs, scratch=(), copies=0, name=None):
    shapes = [pltpu.VMEM(s, d) for s, d in scratch]
    if copies:
        shapes.append(pltpu.SemaphoreType.DMA((copies,)))
    return pl.pallas_call(
        kernel,
        out_shape=[jax.ShapeDtypeStruct(s, d) for s, d in outs],
        in_specs=in_specs,
        out_specs=[VMEM] * len(outs),
        scratch_shapes=shapes,
        name=name,
    )


def edges_of():
    place = lax.axis_index("rows")
    return (place == 0, place == lax.axis_size("rows") - 1)


def coefficient(times_ref, step):
    stamp = jnp.full((LAT8, 128), times_ref[step], jnp.int32)
    return (stamp.astype(F32) + 1.0) / 1000.0


def prep_kernel(gated_ref, enc_ref, dec_ref, down_ref, tmid_ref, time_ref, enc_out, dec_out, down_out, tmid_out, bias_out):
    chans = enc_ref.shape[3]
    for src, dst in ((enc_ref, enc_out), (dec_ref, dec_out)):
        for dy in range(3):
            for dx in range(3):
                dst[dx * chans : (dx + 1) * chans, dy * chans : (dy + 1) * chans] = src[dy, dx].T
    for dy in range(3):
        for dx in range(3):
            lane = (3 * dy + dx) * chans
            down_out[:, lane : lane + chans] = down_ref[dy, dx].T
        tmid_out[dy] = tmid_ref[dy].T
    biases = dot(gated_ref[...], time_ref[...])
    turned = biases.T
    for step in range(bias_out.shape[0]):
        bias_out[step] = jnp.broadcast_to(turned[:, step : step + 1], bias_out.shape[1:])


def spread_rows(acat_ref, row, value, cols, chans):
    for dy in range(3):
        start = pl.multiple_of((row - dy + 2) * cols, cols)
        acat_ref[dy * chans : (dy + 1) * chans, pl.ds(start, cols)] = value


def conv_sum(acc_ref, row, cols, chans):
    span = pl.ds(pl.multiple_of(row * cols, cols), cols)
    return (
        acc_ref[chans : 2 * chans, span]
        + shifted(acc_ref[:chans, span], 1)
        + shifted(acc_ref[2 * chans :, span], -1)
    )


def encode_rows(read_row, w_in, wcat_ref, bias_ref, copies, border, out_ref, lift_ref, acat_ref, acc_ref):
    count, chans, cols = out_ref.shape
    is_first, is_last = edges_of()

    def front(row, carry):
        lifted = lax.dot_general(
            w_in, read_row(row), (((0,), (0,)), ((), ())), preferred_element_type=F32
        )
        lift_ref[row] = lifted
        spread_rows(acat_ref, row, act(lifted).astype(BF16), cols, chans)
        return carry

    lax.fori_loop(0, count + 2, front, 0)
    for copy in copies:
        copy.wait()
    acc_ref[...] = dot(wcat_ref[...], acat_ref[:, 2 * cols : (2 + count) * cols])

    def back(row, carry):
        total = lift_ref[row + 1] + conv_sum(acc_ref, row, cols, chans) + bias_ref[...]
        outside = ((row < border) & is_first) | ((row >= count - border) & is_last)
        out_ref[row] = jnp.where(outside, 0.0, total).astype(BF16)
        return carry

    lax.fori_loop(0, count, back, 0)


def fetches(pairs, sems):
    copies = [pltpu.make_async_copy(s, d, sems.at[i]) for i, (s, d) in enumerate(pairs)]
    for copy in copies:
        copy.start()
    return copies


def enc_first_kernel(
    x_ref, taps_ref, wcat_hbm, bias_hbm, out_ref, wcat_ref, bias_ref, lift_ref, acat_ref, acc_ref, sems
):
    chans = out_ref.shape[1]
    copies = fetches(((wcat_hbm, wcat_ref), (bias_hbm.at[0, :chans], bias_ref)), sems)
    encode_rows(
        lambda row: x_ref[row].astype(BF16), taps_ref[9 * LAT8 :, :], wcat_ref, bias_ref, copies, 2,
        out_ref, lift_ref, acat_ref, acc_ref,
    )


def neighbour(even, one, two, above):
    return jnp.where(even, two, one) if above else jnp.where(even, one, two)


def enc_last_kernel(
    base_ref, near_ref, one_ref, two_ref, taps_ref, wcat_hbm, bias_hbm,
    out_ref, x_ref, ext_ref, wcat_ref, bias_ref, lift_ref, acat_ref, acc_ref, sems,
):
    chans = out_ref.shape[1]
    copies = fetches(((wcat_hbm, wcat_ref), (bias_hbm.at[1, :chans], bias_ref)), sems)
    rows = base_ref.shape[0]
    even = lax.axis_index("rows") % 2 == 0
    is_first, is_last = edges_of()
    packed = one_ref.shape[0] - 2 * TILE

    def received(above):
        high = neighbour(even, one_ref[packed : packed + TILE, :], two_ref[packed : packed + TILE, :], above)
        low = neighbour(even, one_ref[packed + TILE :, :], two_ref[packed + TILE :, :], above)
        both = high.astype(F32) + low.astype(F32)
        return both[:LAT8], both[LAT8:]

    from_up, base_up = received(True)
    from_down, base_down = received(False)
    x_ref[...] = base_ref[...]
    x_ref[0] = x_ref[0] - from_up
    x_ref[rows - 1] = x_ref[rows - 1] - from_down
    ext_ref[0] = jnp.where(is_first, 0.0, base_up - near_ref[0]).astype(BF16)
    ext_ref[rows + 1] = jnp.where(is_last, 0.0, base_down - near_ref[1]).astype(BF16)
    ext_ref[1 : rows + 1] = x_ref[...].astype(BF16)
    encode_rows(
        lambda row: ext_ref[row], taps_ref[9 * LAT8 :, :], wcat_ref, bias_ref, copies, 0,
        out_ref, lift_ref, acat_ref, acc_ref,
    )


def down_rows(read_row, w_ref, bias_ref, copies, low_ref, q_ref, acat_ref, cols):
    half = cols // 2
    low_rows = low_ref.shape[1] // half
    chans = acat_ref.shape[0] // 9
    source = lax.broadcasted_iota(jnp.int32, (cols, 2 * cols), 0)
    target = lax.broadcasted_iota(jnp.int32, (cols, 2 * cols), 1)
    wanted = 2 * (target % half) + target // cols
    pick = jnp.where(source == wanted, 1.0, 0.0).astype(BF16)
    column = lax.broadcasted_iota(jnp.int32, (chans, cols), 1)
    for row in range(2 * low_rows + 1):
        gate = act(read_row(row).astype(F32)).astype(BF16)
        both = dot(gate, pick)
        even, odd = both[:, :cols], both[:, cols:]
        before = jnp.where(column % half == 0, 0.0, pltpu.roll(odd, 1, 1))
        parts = [part.astype(BF16) for part in (before, even, odd)]
        for dy in range(3):
            if (row - dy) % 2 or not 0 <= (row - dy) // 2 < low_rows:
                continue
            low = (row - dy) // 2
            lane = (low % 2) * half
            for dx, part in enumerate(parts):
                start = (3 * dy + dx) * chans
                acat_ref[start : start + chans, low * half : (low + 1) * half] = part[:, lane : lane + half]
    for copy in copies:
        copy.wait()
    low_ref[...] = dot(w_ref[...], acat_ref[...])
    for low in range(0, low_ref.shape[1], cols):
        wide = min(cols, low_ref.shape[1] - low)
        total = low_ref[:, low : low + wide] + bias_ref[:, :wide]
        low_ref[:, low : low + wide] = total
        q_ref[:, low : low + wide] = act(total).astype(BF16)


def down_first_kernel(
    own_ref, got_ref, one_ref, two_ref, far_ref, w_hbm, bias_hbm,
    low_ref, q_ref, enc_ref, mid_ref, w_ref, bias_ref, acat_ref, sems,
):
    count, chans, cols = got_ref.shape
    mid = low_ref.shape[0]
    copies = fetches(((w_hbm, w_ref), (bias_hbm.at[0, chans : chans + mid], bias_ref)), sems)
    segment = lax.axis_index("segment")
    first = segment == 0
    even = lax.axis_index("rows") % 2 == 0
    for row in range(count + 2):
        if 1 <= row <= count:
            own, got = own_ref[0, segment, row - 1], got_ref[row - 1]
        else:
            own = neighbour(even, one_ref[segment, :chans], two_ref[segment, :chans], row == 0)
            got = neighbour(even, far_ref[0, :chans], far_ref[1, :chans], row == 0)
        enc_ref[row] = jnp.where(first, own, got)
        mid_ref[row] = jnp.where(first, got, own)
    down_rows(lambda row: enc_ref[row], w_ref, bias_ref, copies, low_ref, q_ref, acat_ref, cols)


def down_last_kernel(enc_ref, w_hbm, bias_hbm, low_ref, q_ref, w_ref, bias_ref, acat_ref, sems):
    chans, cols = enc_ref.shape[1:]
    mid = low_ref.shape[0]
    copies = fetches(((w_hbm, w_ref), (bias_hbm.at[1, chans : chans + mid], bias_ref)), sems)
    down_rows(lambda row: enc_ref[row + 1], w_ref, bias_ref, copies, low_ref, q_ref, acat_ref, cols)


def raise_rows(low_ref, q_ref, other_ref, w_tmid_ref, w_up_ref):
    far = 2 - 2 * lax.axis_index("segment")
    mixed = low_ref[...] + dot(w_tmid_ref[1], q_ref[...]) + dot(w_tmid_ref[far], other_ref[...])
    return dot(w_up_ref[...], mixed.astype(BF16)).astype(BF16)


def doubling(half, rows):
    source = lax.broadcasted_iota(jnp.int32, (rows * half, 2 * rows * half), 0)
    target = lax.broadcasted_iota(jnp.int32, (rows * half, 2 * rows * half), 1)
    return jnp.where(source == target // 2, 1.0, 0.0).astype(BF16)


def mid_first_kernel(
    low_ref, q_ref, other_ref, w_tmid_ref, w_up_ref, base_ref, near_ref, raised_ref, one_ref, two_ref
):
    raised_ref[...] = raise_rows(low_ref, q_ref, other_ref, w_tmid_ref, w_up_ref)
    rows, _, cols = base_ref.shape
    half = cols // 2
    packed = raised_ref.shape[0] // 2
    start = raised_ref.shape[1] - half
    even = lax.axis_index("rows") % 2 == 0

    def bundle(index, lane, edge):
        piece = raised_ref[:, lane : lane + half]
        sent = jnp.concatenate([near_ref[index], base_ref[edge]], axis=0)
        high = sent.astype(BF16)
        low = (sent - high.astype(F32)).astype(BF16)
        folded = jnp.concatenate([piece[:packed], piece[packed:]], axis=1)
        return jnp.concatenate([folded, high, low], axis=0)

    up = bundle(0, 0, 0)
    down = bundle(1, start, rows - 1)
    one_ref[...] = jnp.where(even, down, up)
    two_ref[...] = jnp.where(even, up, down)


def mid_last_kernel(low_ref, q_ref, other_ref, w_tmid_ref, w_up_ref, out_ref):
    raised = raise_rows(low_ref, q_ref, other_ref, w_tmid_ref, w_up_ref)
    rows, _, cols = out_ref.shape
    half = cols // 2
    wide = dot(raised, doubling(half, rows // 2)).astype(BF16)
    for row in range(rows):
        low = row // 2
        out_ref[row] = wide[:, low * cols : (low + 1) * cols]


def decode_rows(count, cols, wcat_ref, w_skip_ref, bias_ref, copies, border, taps_ref, jcat_ref, mixed_ref, acat_ref, acc_ref, o_ref):
    chans = bias_ref.shape[0]
    is_first, is_last = edges_of()
    mixed_ref[...] = dot(w_skip_ref[...], jcat_ref[...])

    def front(row, carry):
        mixed = mixed_ref[:, pl.ds(pl.multiple_of(row * cols, cols), cols)]
        spread_rows(acat_ref, row, act(mixed).astype(BF16), cols, chans)
        return carry

    lax.fori_loop(0, count + 2, front, 0)
    for copy in copies:
        copy.wait()
    acc_ref[...] = dot(wcat_ref[...], acat_ref[:, 2 * cols : (2 + count) * cols])

    def back(row, carry):
        mixed = mixed_ref[:, pl.ds(pl.multiple_of((row + 1) * cols, cols), cols)]
        value = act(mixed + conv_sum(acc_ref, row, cols, chans) + bias_ref[...])
        outside = ((row < border) & is_first) | ((row >= count - border) & is_last)
        span = pl.ds(pl.multiple_of(row * cols, cols), cols)
        o_ref[:, span] = jnp.where(outside, 0.0, value).astype(BF16)
        return carry

    lax.fori_loop(0, count, back, 0)
    taps = dot(taps_ref[: 9 * LAT8, :], o_ref[...])
    span = 3 * LAT8
    parts = []
    for row in range(count):
        tap = taps[:, row * cols : (row + 1) * cols]
        parts.append(shifted(tap[:span], 1) + tap[span : 2 * span] + shifted(tap[2 * span :], -1))
    return parts


def tap_sum(parts, row):
    total = None
    for dy in range(3):
        source = row + dy - 1
        if 0 <= source < len(parts):
            piece = parts[source][dy * LAT8 : (dy + 1) * LAT8]
            total = piece if total is None else total + piece
    return total


def dec_first_kernel(
    times_ref, enc_ref, mid_ref, x_ref, w_skip_ref, taps_ref, wcat_hbm, bias_hbm,
    base_ref, near_ref, jcat_ref, wcat_ref, bias_ref, mixed_ref, acat_ref, acc_ref, o_ref, sems,
):
    rows = base_ref.shape[0]
    chans, cols = enc_ref.shape[1:]
    start = bias_hbm.shape[1] - chans
    copies = fetches(((wcat_hbm, wcat_ref), (bias_hbm.at[0, start:], bias_ref)), sems)
    for row in range(rows + 2):
        jcat_ref[:chans, row * cols : (row + 1) * cols] = mid_ref[row]
        jcat_ref[chans:, row * cols : (row + 1) * cols] = enc_ref[row]
    parts = decode_rows(
        rows, cols, wcat_ref, w_skip_ref, bias_ref, copies, 0, taps_ref, jcat_ref, mixed_ref, acat_ref, acc_ref, o_ref
    )
    coef = coefficient(times_ref, 0)
    halo = (x_ref.shape[0] - rows) // 2
    near_ref[0] = coef * tap_sum(parts, -1)
    near_ref[1] = coef * tap_sum(parts, rows)
    for row in range(rows):
        base_ref[row] = x_ref[halo + row] - coef * tap_sum(parts, row)


def dec_last_kernel(
    times_ref, enc_ref, mid_ref, one_ref, two_ref, x_ref, w_skip_ref, taps_ref, wcat_hbm, bias_hbm,
    next_ref, jcat_ref, wcat_ref, bias_ref, mixed_ref, acat_ref, acc_ref, o_ref, sems,
):
    rows = x_ref.shape[0]
    chans, cols = enc_ref.shape[1:]
    start = bias_hbm.shape[1] - chans
    copies = fetches(((wcat_hbm, wcat_ref), (bias_hbm.at[1, start:], bias_ref)), sems)
    half = cols // 2
    inner = rows // 2
    even = lax.axis_index("rows") % 2 == 0
    packed = chans // 2
    wide = dot(mid_ref[...], doubling(half, inner)).astype(BF16)
    twice = doubling(half, 1)
    for low in range(inner + 2):
        if 1 <= low <= inner:
            piece = wide[:, (low - 1) * cols : low * cols]
        else:
            folded = neighbour(even, one_ref[:packed, :], two_ref[:packed, :], low == 0)
            piece = dot(jnp.concatenate([folded[:, :half], folded[:, half:]], axis=0), twice).astype(BF16)
        for row in (2 * low, 2 * low + 1):
            jcat_ref[:chans, row * cols : (row + 1) * cols] = piece
            jcat_ref[chans:, row * cols : (row + 1) * cols] = enc_ref[row]
    parts = decode_rows(
        rows + 2, cols, wcat_ref, w_skip_ref, bias_ref, copies, 1, taps_ref, jcat_ref, mixed_ref, acat_ref, acc_ref, o_ref
    )
    coef = coefficient(times_ref, 1)
    for row in range(rows):
        next_ref[row] = x_ref[row] - coef * tap_sum(parts, row + 1)


def gated_times(timesteps, half):
    freqs = jnp.exp(-math.log(10000.0) * jnp.arange(half).astype(F32) / half)
    angles = timesteps.astype(F32)[:, None] * freqs[None, :]
    embedded = jnp.concatenate([jnp.sin(angles), jnp.cos(angles)], axis=1)
    gated = jax.nn.silu(embedded).astype(BF16)
    return jnp.pad(gated, ((0, TILE - gated.shape[0]), (0, 0)))


def body(latent, stale, timesteps, w_in, w_enc, w_down, w_tmid, w_up, w_skip, w_dec, w_out, w_time):
    segment = lax.axis_index("segment")
    first = segment == 0
    size = lax.axis_size("rows")
    even = lax.axis_index("rows") % 2 == 0
    chan_major = stale.transpose(0, 1, 2, 4, 3)
    state = chan_major[0]
    frames, rows, chans, cols = state.shape
    mid = w_down.shape[3]
    lat = w_in.shape[0]
    half = cols // 2
    low = (rows // 2) * half
    halo = 3
    assert frames == 2 and lax.axis_size("segment") == 2

    def paired(start):
        return [p for i in range(start, size - 1, 2) for p in ((i, i + 1), (i + 1, i))]

    def swap(value):
        return lax.ppermute(value, "segment", [(0, 1), (1, 0)])

    def exchange(one, two):
        return lax.ppermute(one, "rows", paired(0)), lax.ppermute(two, "rows", paired(1))

    def mine(value, axis=0):
        return lax.dynamic_index_in_dim(value, segment, axis, keepdims=False)

    def theirs(value, axis=0):
        return lax.dynamic_index_in_dim(value, 1 - segment, axis, keepdims=False)

    def edge_rows(state_rows, latent_rows):
        flat = latent_rows.astype(BF16).reshape(frames, -1, cols)
        spare = -flat.shape[1] % TILE
        return jnp.concatenate([state_rows, jnp.pad(flat, ((0, 0), (0, spare), (0, 0)))], axis=1)

    last = edge_rows(state[:, rows - 1], latent[:, rows - halo :])
    top = edge_rows(state[:, 0], latent[:, :halo])
    one, two = exchange(jnp.where(even, last, top), jnp.where(even, top, last))
    got = swap(theirs(state))
    x_got = swap(theirs(latent))
    far = swap(jnp.stack([theirs(one), theirs(two)]))

    def latent_rows(piece):
        return piece[chans : chans + halo * latent.shape[2] // cols].reshape(halo, latent.shape[2]).astype(F32)

    def columns(own, one_piece, two_piece):
        above = jnp.where(even, two_piece, one_piece)
        below = jnp.where(even, one_piece, two_piece)
        return jnp.concatenate([latent_rows(above), own, latent_rows(below)], axis=0)

    near_cols = columns(mine(latent), mine(one), mine(two))
    far_cols = columns(x_got, far[0], far[1])
    x_full = jnp.concatenate(
        [jnp.where(first, near_cols, far_cols), jnp.where(first, far_cols, near_cols)], axis=1
    )
    x_t = x_full.reshape(rows + 2 * halo, cols, lat).transpose(0, 2, 1)
    x_t = jnp.pad(x_t, ((0, 0), (0, LAT8 - lat), (0, 0)))

    taps = jnp.pad(w_out.transpose(1, 0, 3, 2), ((0, 0), (0, 0), (0, LAT8 - lat), (0, 0)))
    taps = jnp.concatenate(
        [taps.reshape(9 * LAT8, chans), jnp.pad(w_in, ((0, LAT8 - lat), (0, 0)))], axis=0
    )
    w_up_t = w_up.T
    w_skip_t = w_skip.T
    wide = 3 * chans
    total = w_time.shape[1]

    enc_cat, dec_cat, w_down_t, w_tmid_t, bias = call(
        prep_kernel,
        [
            ((wide, wide), BF16),
            ((wide, wide), BF16),
            ((mid, 3 * wide), BF16),
            ((3, mid, mid), BF16),
            ((timesteps.shape[0], total, cols), F32),
        ],
        [VMEM] * 6,
        name="prep",
    )(gated_times(timesteps, w_time.shape[0] // 2), w_enc, w_dec, w_down, w_tmid, w_time)

    def enc_scratch(count):
        return [
            ((wide, wide), BF16),
            ((chans, cols), F32),
            ((count + 2, chans, cols), F32),
            ((wide, (count + 4) * cols), BF16),
            ((wide, count * cols), F32),
        ]

    def dec_scratch(count):
        return [
            ((2 * chans, (count + 2) * cols), BF16),
            ((wide, wide), BF16),
            ((chans, cols), F32),
            ((chans, (count + 2) * cols), F32),
            ((wide, (count + 4) * cols), BF16),
            ((wide, count * cols), F32),
            ((chans, count * cols), BF16),
        ]

    down_scratch = [((mid, 3 * wide), BF16), ((mid, cols), F32), ((3 * wide, low), BF16)]
    down_outs = [((mid, low), F32), ((mid, low), BF16)]
    ext = ((rows + 2, chans, cols), BF16)
    low0, q0, enc0, mid0 = call(
        down_first_kernel, down_outs + [ext, ext], [VMEM] * 5 + [ANY] * 2, down_scratch, 2, "down_first"
    )(chan_major, got, one, two, far, w_down_t, bias)
    q0_other = swap(q0)

    (enc1,) = call(
        enc_first_kernel,
        [((rows + 4, chans, cols), BF16)],
        [VMEM] * 2 + [ANY] * 2,
        enc_scratch(rows + 4),
        2,
        "enc_first",
    )(x_t, taps, enc_cat, bias)

    base, near = call(
        dec_first_kernel,
        [((rows, LAT8, cols), F32), ((2, LAT8, cols), F32)],
        [SMEM] + [VMEM] * 5 + [ANY] * 2,
        dec_scratch(rows),
        2,
        "dec_first",
    )(timesteps, enc0, mid0, x_t, w_skip_t, taps, dec_cat, bias)

    bundle = ((chans // 2 + 2 * TILE, cols), BF16)
    mid1, to_one, to_two = call(
        mid_first_kernel, [((chans, low), BF16), bundle, bundle], [VMEM] * 7, name="mid_first"
    )(low0, q0, q0_other, w_tmid_t, w_up_t, base, near)
    got_one, got_two = exchange(to_one, to_two)

    low1, q1 = call(
        down_last_kernel, down_outs, [VMEM] + [ANY] * 2, down_scratch, 2, "down_last"
    )(enc1, w_down_t, bias)
    q1_other = swap(q1)

    (mid2,) = call(mid_last_kernel, [((rows, chans, cols), BF16)], [VMEM] * 5, name="mid_last")(
        low1, q1, q1_other, w_tmid_t, w_up_t
    )

    enc2, x1 = call(
        enc_last_kernel,
        [((rows, chans, cols), BF16), ((rows, LAT8, cols), F32)],
        [VMEM] * 5 + [ANY] * 2,
        [((rows + 2, LAT8, cols), BF16)] + enc_scratch(rows),
        2,
        "enc_last",
    )(base, near, got_one, got_two, taps, enc_cat, bias)

    feat_other = swap(jnp.where(first, mid2, enc2))

    (x2,) = call(
        dec_last_kernel,
        [((rows, LAT8, cols), F32)],
        [SMEM] + [VMEM] * 7 + [ANY] * 2,
        dec_scratch(rows + 2),
        2,
        "dec_last",
    )(timesteps, enc1, mid1, got_one, got_two, x1, w_skip_t, taps, dec_cat, bias)

    flat = x2[:, :lat].transpose(0, 2, 1).reshape(rows, cols * lat)
    halves = jnp.stack([flat[:, : cols * lat // 2], flat[:, cols * lat // 2 :]])
    x_keep, x_far = mine(halves), swap(theirs(halves))
    result = jnp.where(first, jnp.stack([x_keep, x_far]), jnp.stack([x_far, x_keep]))
    features = jnp.where(first, jnp.stack([enc2, feat_other]), jnp.stack([feat_other, mid2]))
    return (result, features.transpose(0, 1, 3, 2)[None])


def solution(mesh):
    placed = (
        P("clips", "rows", "segment"),
        P("segment", "clips", "rows", None, None),
        P("clips"),
    ) + (P(),) * 9
    return jax.shard_map(
        body,
        mesh=mesh,
        in_specs=placed,
        out_specs=(P("clips", "rows", "segment"), P("segment", "clips", "rows", None, None)),
        check_vma=False,
    )
```

```python
import math

import jax
import jax.numpy as jnp
from jax import lax
from jax.experimental import pallas as pl
from jax.experimental.pallas import tpu as pltpu
from jax.sharding import PartitionSpec as P


EPSILON = 1e-06
LAT8 = 8
TILE = 16
F32 = jnp.float32
BF16 = jnp.bfloat16

VMEM = pl.BlockSpec(memory_space=pltpu.VMEM)
SMEM = pl.BlockSpec(memory_space=pltpu.SMEM)
ANY = pl.BlockSpec(memory_space=pl.ANY)


def act(values):
    scale = lax.rsqrt(jnp.mean(values * values, axis=0, keepdims=True) + EPSILON)
    half = values * (0.5 * scale)
    return half + half * jnp.tanh(half)


def dot(left, right):
    return jnp.dot(left, right, preferred_element_type=F32)


def shifted(values, by):
    count = values.shape[1]
    column = lax.broadcasted_iota(jnp.int32, values.shape, 1)
    edge = 0 if by == 1 else count - 1
    return jnp.where(column == edge, 0.0, pltpu.roll(values, by % count, 1))


def call(kernel, outs, in_specs, scratch=(), copies=0, out_specs=None):
    shapes = [pltpu.VMEM(s, d) for s, d in scratch]
    if copies:
        shapes.append(pltpu.SemaphoreType.DMA((copies,)))
    return pl.pallas_call(
        kernel,
        out_shape=[jax.ShapeDtypeStruct(s, d) for s, d in outs],
        in_specs=in_specs,
        out_specs=out_specs or [VMEM] * len(outs),
        scratch_shapes=shapes,
    )


def edges_of():
    place = lax.axis_index("rows")
    return (place == 0, place == lax.axis_size("rows") - 1)


def coefficient(times_ref, step):
    stamp = jnp.full((LAT8, 128), times_ref[step], jnp.int32)
    return (stamp.astype(F32) + 1.0) / 1000.0


def fetches(pairs, sems):
    copies = [pltpu.make_async_copy(s, d, sems.at[i]) for i, (s, d) in enumerate(pairs)]
    for copy in copies:
        copy.start()
    return copies


def prep_kernel(
    gated_ref, enc_hbm, dec_hbm, down_hbm, tmid_hbm, time_hbm,
    enc_out, dec_out, down_out, tmid_out, bias_out,
    enc_ref, dec_ref, down_ref, tmid_ref, time_ref, enc_t, dec_t, down_t, tmid_t, bias_t, sems,
):
    pairs = []
    for hbm, ref in ((enc_hbm, enc_ref), (dec_hbm, dec_ref), (down_hbm, down_ref)):
        pairs += [(hbm.at[dy], ref.at[dy]) for dy in range(3)]
    pairs += [(tmid_hbm.at[k], tmid_ref.at[k]) for k in range(3)] + [(time_hbm, time_ref)]
    copies = fetches(pairs, sems)
    count = len(pairs)
    outs = []

    def send(src, dst):
        copy = pltpu.make_async_copy(src, dst, sems.at[count + len(outs)])
        copy.start()
        outs.append(copy)

    arrived = iter(copies)
    for src, turned, dst in ((enc_ref, enc_t, enc_out), (dec_ref, dec_t, dec_out), (down_ref, down_t, down_out)):
        chans = src.shape[2]
        for dy in range(3):
            next(arrived).wait()
            for dx in range(3):
                lane = (3 * dy + dx) * chans
                turned[:, lane : lane + chans] = src[dy, dx].T
        send(turned, dst)
    for k in range(3):
        next(arrived).wait()
        tmid_t[k] = tmid_ref[k].T
        send(tmid_t.at[k], tmid_out.at[k])
    next(arrived).wait()
    biases = dot(gated_ref[...], time_ref[...]).T
    for step in range(bias_t.shape[0]):
        bias_t[step] = jnp.broadcast_to(biases[:, step : step + 1], bias_t.shape[1:])
    send(bias_t, bias_out)
    for copy in outs:
        copy.wait()


def store_taps(taps_ref, row, value):
    chans, cols = value.shape
    span = slice(row * cols, (row + 1) * cols)
    taps_ref[:chans, span] = shifted(value, 1).astype(BF16)
    taps_ref[chans : 2 * chans, span] = value.astype(BF16)
    taps_ref[2 * chans :, span] = shifted(value, -1).astype(BF16)


def conv_pairs(count, cols, front, back, w_ref, taps_ref, acc_ref, copies):
    front(0)
    front(2)
    for copy in copies:
        copy.wait()
    for pair in range(0, count, 2):
        window = jnp.concatenate(
            [taps_ref[:, (pair + dy) * cols : (pair + dy + 2) * cols] for dy in range(3)], axis=0
        )
        acc_ref[:, pair * cols : (pair + 2) * cols] = dot(w_ref[...], window)
        if pair + 4 <= count:
            front(pair + 4)
        if pair:
            back(pair - 2)
    back(count - 2)


def encode_rows(read_pair, w_in, w_ref, bias_ref, copies, border, out_ref, lift_ref, taps_ref, acc_ref):
    count, _, cols = out_ref.shape
    is_first, is_last = edges_of()

    def front(row):
        lifted = dot(w_in, read_pair(row))
        lift_ref[:, row * cols : (row + 2) * cols] = lifted
        for k in range(2):
            store_taps(taps_ref, row + k, act(lifted[:, k * cols : (k + 1) * cols]))

    def back(pair):
        for row in (pair, pair + 1):
            here = slice(row * cols, (row + 1) * cols)
            there = slice((row + 1) * cols, (row + 2) * cols)
            total = lift_ref[:, there] + acc_ref[:, here] + bias_ref[...]
            if row < border:
                total = jnp.where(is_first, 0.0, total)
            if row >= count - border:
                total = jnp.where(is_last, 0.0, total)
            out_ref[row] = total.astype(BF16)

    conv_pairs(count, cols, front, back, w_ref, taps_ref, acc_ref, copies)


def turned_w_in(w_small_ref):
    return w_small_ref[9 * LAT8 :, :].astype(F32).T.astype(BF16)


def enc_first_kernel(
    x_ref, w_small_ref, w_hbm, bias_hbm, out_ref, w_ref, bias_ref, lift_ref, taps_ref, acc_ref, sems
):
    chans = out_ref.shape[1]
    copies = fetches(((w_hbm, w_ref), (bias_hbm.at[0, :chans], bias_ref)), sems)
    encode_rows(
        lambda row: jnp.concatenate([x_ref[row], x_ref[row + 1]], axis=1).astype(BF16),
        turned_w_in(w_small_ref), w_ref, bias_ref, copies, 2, out_ref, lift_ref, taps_ref, acc_ref,
    )


def neighbour(even, one, two, above):
    return jnp.where(even, two, one) if above else jnp.where(even, one, two)


def enc_last_kernel(
    base_ref, near_ref, one_ref, two_ref, w_small_ref, w_hbm, bias_hbm,
    out_ref, x_ref, w_ref, bias_ref, lift_ref, taps_ref, acc_ref, sems,
):
    chans = out_ref.shape[1]
    copies = fetches(((w_hbm, w_ref), (bias_hbm.at[1, :chans], bias_ref)), sems)
    rows = base_ref.shape[0]
    even = lax.axis_index("rows") % 2 == 0
    is_first, is_last = edges_of()
    packed = one_ref.shape[0] - 2 * TILE

    def received(above):
        high = neighbour(even, one_ref[packed : packed + TILE, :], two_ref[packed : packed + TILE, :], above)
        low = neighbour(even, one_ref[packed + TILE :, :], two_ref[packed + TILE :, :], above)
        both = high.astype(F32) + low.astype(F32)
        return both[:LAT8], both[LAT8:]

    from_up, base_up = received(True)
    from_down, base_down = received(False)
    ext = [base_ref[row] for row in range(rows)]
    ext[0] = ext[0] - from_up
    ext[-1] = ext[-1] - from_down
    for row in range(rows):
        x_ref[row] = ext[row]
    ext = (
        [jnp.where(is_first, 0.0, base_up - near_ref[0])]
        + ext
        + [jnp.where(is_last, 0.0, base_down - near_ref[1])]
    )
    encode_rows(
        lambda row: jnp.concatenate(ext[row : row + 2], axis=1).astype(BF16),
        turned_w_in(w_small_ref), w_ref, bias_ref, copies, 0, out_ref, lift_ref, taps_ref, acc_ref,
    )


def down_rows(read_row, w_ref, bias_ref, copies, low_ref, q_ref, acat_ref, cols):
    half = cols // 2
    low_rows = low_ref.shape[1] // half
    chans = acat_ref.shape[0] // 9
    source = lax.broadcasted_iota(jnp.int32, (cols, 2 * cols), 0)
    target = lax.broadcasted_iota(jnp.int32, (cols, 2 * cols), 1)
    wanted = 2 * (target % half) + target // cols
    pick = jnp.where(source == wanted, 1.0, 0.0).astype(BF16)
    column = lax.broadcasted_iota(jnp.int32, (chans, cols), 1)
    for row in range(2 * low_rows + 1):
        gate = act(read_row(row).astype(F32)).astype(BF16)
        both = dot(gate, pick)
        even, odd = both[:, :cols], both[:, cols:]
        before = jnp.where(column % half == 0, 0.0, pltpu.roll(odd, 1, 1))
        parts = [part.astype(BF16) for part in (before, even, odd)]
        for dy in range(3):
            if (row - dy) % 2 or not 0 <= (row - dy) // 2 < low_rows:
                continue
            low = (row - dy) // 2
            lane = (low % 2) * half
            for dx, part in enumerate(parts):
                start = (3 * dy + dx) * chans
                acat_ref[start : start + chans, low * half : (low + 1) * half] = part[:, lane : lane + half]
    for copy in copies:
        copy.wait()
    low_ref[...] = dot(w_ref[...], acat_ref[...])
    for low in range(0, low_ref.shape[1], cols):
        wide = min(cols, low_ref.shape[1] - low)
        total = low_ref[:, low : low + wide] + bias_ref[:, :wide]
        low_ref[:, low : low + wide] = total
        q_ref[:, low : low + wide] = act(total).astype(BF16)


def down_first_kernel(
    own_ref, got_ref, one_ref, two_ref, far_ref, w_hbm, bias_hbm,
    low_ref, q_ref, enc_ref, mid_ref, w_ref, bias_ref, acat_ref, sems,
):
    count, chans, cols = got_ref.shape
    mid = low_ref.shape[0]
    copies = fetches(((w_hbm, w_ref), (bias_hbm.at[0, chans : chans + mid], bias_ref)), sems)
    segment = lax.axis_index("segment")
    first = segment == 0
    even = lax.axis_index("rows") % 2 == 0
    for row in range(count + 2):
        if 1 <= row <= count:
            own, got = own_ref[0, segment, row - 1], got_ref[row - 1]
        else:
            own = neighbour(even, one_ref[segment, :chans], two_ref[segment, :chans], row == 0)
            got = neighbour(even, far_ref[0, :chans], far_ref[1, :chans], row == 0)
        enc_ref[row] = jnp.where(first, own, got)
        mid_ref[row] = jnp.where(first, got, own)
    down_rows(lambda row: enc_ref[row], w_ref, bias_ref, copies, low_ref, q_ref, acat_ref, cols)


def down_last_kernel(enc_ref, w_hbm, bias_hbm, low_ref, q_ref, w_ref, bias_ref, acat_ref, sems):
    chans, cols = enc_ref.shape[1:]
    mid = low_ref.shape[0]
    copies = fetches(((w_hbm, w_ref), (bias_hbm.at[1, chans : chans + mid], bias_ref)), sems)
    down_rows(lambda row: enc_ref[row + 1], w_ref, bias_ref, copies, low_ref, q_ref, acat_ref, cols)


def raise_rows(low_ref, q_ref, other_ref, w_tmid_ref, w_up_ref):
    far = 2 - 2 * lax.axis_index("segment")
    mixed = low_ref[...] + dot(w_tmid_ref[1], q_ref[...]) + dot(w_tmid_ref[far], other_ref[...])
    return dot(w_up_ref[...], mixed.astype(BF16)).astype(BF16)


def doubling(half, rows):
    source = lax.broadcasted_iota(jnp.int32, (rows * half, 2 * rows * half), 0)
    target = lax.broadcasted_iota(jnp.int32, (rows * half, 2 * rows * half), 1)
    return jnp.where(source == target // 2, 1.0, 0.0).astype(BF16)


def mid_first_kernel(
    low_ref, q_ref, other_ref, w_tmid_ref, w_up_ref, base_ref, near_ref, raised_ref, one_ref, two_ref
):
    raised_ref[...] = raise_rows(low_ref, q_ref, other_ref, w_tmid_ref, w_up_ref)
    rows, _, cols = base_ref.shape
    half = cols // 2
    packed = raised_ref.shape[0] // 2
    start = raised_ref.shape[1] - half
    even = lax.axis_index("rows") % 2 == 0

    def bundle(index, lane, edge):
        piece = raised_ref[:, lane : lane + half]
        sent = jnp.concatenate([near_ref[index], base_ref[edge]], axis=0)
        high = sent.astype(BF16)
        low = (sent - high.astype(F32)).astype(BF16)
        folded = jnp.concatenate([piece[:packed], piece[packed:]], axis=1)
        return jnp.concatenate([folded, high, low], axis=0)

    up = bundle(0, 0, 0)
    down = bundle(1, start, rows - 1)
    one_ref[...] = jnp.where(even, down, up)
    two_ref[...] = jnp.where(even, up, down)


def mid_last_kernel(low_ref, q_ref, other_ref, w_tmid_ref, w_up_ref, out_ref):
    raised = raise_rows(low_ref, q_ref, other_ref, w_tmid_ref, w_up_ref)
    rows, _, cols = out_ref.shape
    half = cols // 2
    wide = dot(raised, doubling(half, rows // 2)).astype(BF16)
    for row in range(rows):
        low = row // 2
        out_ref[row] = wide[:, low * cols : (low + 1) * cols]


def decode_rows(count, cols, read_joined, w_ref, w_skip_ref, bias_ref, copies, border, w_small_ref, mixed_ref, taps_ref, acc_ref):
    is_first, is_last = edges_of()
    span = 3 * LAT8
    parts = []

    def front(row):
        mixed = dot(w_skip_ref[...], jnp.concatenate([read_joined(row), read_joined(row + 1)], axis=1))
        mixed_ref[:, row * cols : (row + 2) * cols] = mixed
        for k in range(2):
            store_taps(taps_ref, row + k, act(mixed[:, k * cols : (k + 1) * cols]))

    def back(pair):
        outs = []
        for row in (pair, pair + 1):
            here = slice(row * cols, (row + 1) * cols)
            there = slice((row + 1) * cols, (row + 2) * cols)
            value = act(mixed_ref[:, there] + acc_ref[:, here] + bias_ref[...])
            if row < border:
                value = jnp.where(is_first, 0.0, value)
            if row >= count - border:
                value = jnp.where(is_last, 0.0, value)
            outs.append(value.astype(BF16))
        taps = dot(w_small_ref[: 9 * LAT8, :], jnp.concatenate(outs, axis=1))
        for k in range(2):
            tap = taps[:, k * cols : (k + 1) * cols]
            parts.append(shifted(tap[:span], 1) + tap[span : 2 * span] + shifted(tap[2 * span :], -1))

    conv_pairs(count, cols, front, back, w_ref, taps_ref, acc_ref, copies)
    return parts


def tap_sum(parts, row):
    total = None
    for dy in range(3):
        source = row + dy - 1
        if 0 <= source < len(parts):
            piece = parts[source][dy * LAT8 : (dy + 1) * LAT8]
            total = piece if total is None else total + piece
    return total


def dec_first_kernel(
    times_ref, enc_ref, mid_ref, x_ref, w_skip_ref, w_small_ref, w_hbm, bias_hbm,
    base_ref, near_ref, w_ref, bias_ref, mixed_ref, taps_ref, acc_ref, sems,
):
    rows = base_ref.shape[0]
    chans, cols = enc_ref.shape[1:]
    start = bias_hbm.shape[1] - chans
    copies = fetches(((w_hbm, w_ref), (bias_hbm.at[0, start:], bias_ref)), sems)
    parts = decode_rows(
        rows, cols, lambda row: jnp.concatenate([mid_ref[row], enc_ref[row]], axis=0),
        w_ref, w_skip_ref, bias_ref, copies, 0, w_small_ref, mixed_ref, taps_ref, acc_ref,
    )
    coef = coefficient(times_ref, 0)
    halo = (x_ref.shape[0] - rows) // 2
    near_ref[0] = coef * tap_sum(parts, -1)
    near_ref[1] = coef * tap_sum(parts, rows)
    for row in range(rows):
        base_ref[row] = x_ref[halo + row] - coef * tap_sum(parts, row)


def dec_last_kernel(
    times_ref, enc_ref, mid_ref, one_ref, two_ref, x_ref, w_skip_ref, w_small_ref, w_hbm, bias_hbm,
    next_ref, wide_ref, w_ref, bias_ref, mixed_ref, taps_ref, acc_ref, sems,
):
    rows = x_ref.shape[0]
    chans, cols = enc_ref.shape[1:]
    start = bias_hbm.shape[1] - chans
    copies = fetches(((w_hbm, w_ref), (bias_hbm.at[1, start:], bias_ref)), sems)
    half = cols // 2
    inner = rows // 2
    even = lax.axis_index("rows") % 2 == 0
    packed = chans // 2
    wide_ref[:, cols : (inner + 1) * cols] = dot(mid_ref[...], doubling(half, inner)).astype(BF16)
    twice = doubling(half, 1)
    for low in (0, inner + 1):
        folded = neighbour(even, one_ref[:packed, :], two_ref[:packed, :], low == 0)
        piece = jnp.concatenate([folded[:, :half], folded[:, half:]], axis=0)
        wide_ref[:, low * cols : (low + 1) * cols] = dot(piece, twice).astype(BF16)

    def joined(row):
        low = row // 2
        return jnp.concatenate([wide_ref[:, low * cols : (low + 1) * cols], enc_ref[row]], axis=0)

    parts = decode_rows(
        rows + 2, cols, joined, w_ref, w_skip_ref, bias_ref, copies, 1, w_small_ref, mixed_ref, taps_ref, acc_ref
    )
    coef = coefficient(times_ref, 1)
    for row in range(rows):
        next_ref[row] = x_ref[row] - coef * tap_sum(parts, row + 1)


def gated_times(timesteps, half):
    freqs = jnp.exp(-math.log(10000.0) * jnp.arange(half).astype(F32) / half)
    angles = timesteps.astype(F32)[:, None] * freqs[None, :]
    embedded = jnp.concatenate([jnp.sin(angles), jnp.cos(angles)], axis=1)
    gated = jax.nn.silu(embedded).astype(BF16)
    return jnp.pad(gated, ((0, TILE - gated.shape[0]), (0, 0)))


def step_pair(latent, stale, timesteps, w_in, w_enc, w_down, w_tmid, w_up, w_skip, w_dec, w_out, w_time):
    segment = lax.axis_index("segment")
    first = segment == 0
    size = lax.axis_size("rows")
    even = lax.axis_index("rows") % 2 == 0
    chan_major = stale.transpose(0, 1, 2, 4, 3)
    state = chan_major[0]
    frames, rows, chans, cols = state.shape
    mid = w_down.shape[3]
    lat = w_in.shape[0]
    half = cols // 2
    low = (rows // 2) * half
    halo = 3
    assert frames == 2 and lax.axis_size("segment") == 2

    def paired(start):
        return [p for i in range(start, size - 1, 2) for p in ((i, i + 1), (i + 1, i))]

    def swap(value):
        return lax.ppermute(value, "segment", [(0, 1), (1, 0)])

    def exchange(one, two):
        got_one = lax.ppermute(one, "rows", paired(0))
        got_two = lax.ppermute(two, "rows", paired(1))
        return got_one, got_two

    def mine(value, axis=0):
        return lax.dynamic_index_in_dim(value, segment, axis, keepdims=False)

    def theirs(value, axis=0):
        return lax.dynamic_index_in_dim(value, 1 - segment, axis, keepdims=False)

    def edge_rows(state_rows, latent_rows):
        flat = latent_rows.astype(BF16).reshape(frames, -1, cols)
        spare = -flat.shape[1] % TILE
        return jnp.concatenate([state_rows, jnp.pad(flat, ((0, 0), (0, spare), (0, 0)))], axis=1)

    last = edge_rows(state[:, rows - 1], latent[:, rows - halo :])
    top = edge_rows(state[:, 0], latent[:, :halo])
    one, two = exchange(jnp.where(even, last, top), jnp.where(even, top, last))
    got = swap(theirs(state))
    x_got = swap(theirs(latent))
    far = swap(jnp.stack([theirs(one), theirs(two)]))

    def latent_rows(piece):
        return piece[chans : chans + halo * latent.shape[2] // cols].reshape(halo, latent.shape[2]).astype(F32)

    def columns(own, one_piece, two_piece):
        above = jnp.where(even, two_piece, one_piece)
        below = jnp.where(even, one_piece, two_piece)
        return jnp.concatenate([latent_rows(above), own, latent_rows(below)], axis=0)

    near_cols = columns(mine(latent), mine(one), mine(two))
    far_cols = columns(x_got, far[0], far[1])
    x_full = jnp.concatenate(
        [jnp.where(first, near_cols, far_cols), jnp.where(first, far_cols, near_cols)], axis=1
    )
    x_t = x_full.reshape(rows + 2 * halo, cols, lat).transpose(0, 2, 1)
    x_t = jnp.pad(x_t, ((0, 0), (0, LAT8 - lat), (0, 0)))

    taps = jnp.pad(w_out.transpose(1, 0, 3, 2), ((0, 0), (0, 0), (0, LAT8 - lat), (0, 0)))
    taps = jnp.concatenate(
        [taps.reshape(9 * LAT8, chans), jnp.pad(w_in, ((0, LAT8 - lat), (0, 0)))], axis=0
    )
    w_up_t = w_up.T
    w_skip_t = w_skip.T
    wide = 3 * chans
    total = w_time.shape[1]

    turned = [
        ((chans, 3 * wide), BF16),
        ((chans, 3 * wide), BF16),
        ((mid, 3 * wide), BF16),
        ((3, mid, mid), BF16),
        ((timesteps.shape[0], total, cols), F32),
    ]
    weights = (w_enc, w_dec, w_down, w_tmid, w_time)
    gated = gated_times(timesteps, w_time.shape[0] // 2)
    enc_cat, dec_cat, w_down_t, w_tmid_t, bias = call(
        prep_kernel, turned, [VMEM] + [ANY] * 5, [(w.shape, BF16) for w in weights] + turned, 20, [ANY] * 5
    )(gated, *weights)

    def enc_scratch(count):
        return [
            ((chans, 3 * wide), BF16),
            ((chans, cols), F32),
            ((chans, (count + 2) * cols), F32),
            ((wide, (count + 2) * cols), BF16),
            ((chans, count * cols), F32),
        ]

    dec_scratch = enc_scratch
    down_scratch = [((mid, 3 * wide), BF16), ((mid, cols), F32), ((3 * wide, low), BF16)]
    down_outs = [((mid, low), F32), ((mid, low), BF16)]
    ext = ((rows + 2, chans, cols), BF16)
    low0, q0, enc0, mid0 = call(
        down_first_kernel, down_outs + [ext, ext], [VMEM] * 5 + [ANY] * 2, down_scratch, 2
    )(chan_major, got, one, two, far, w_down_t, bias)
    q0_other = swap(q0)

    (enc1,) = call(
        enc_first_kernel, [((rows + 4, chans, cols), BF16)], [VMEM] * 2 + [ANY] * 2, enc_scratch(rows + 4), 2
    )(x_t, taps, enc_cat, bias)

    base, near = call(
        dec_first_kernel,
        [((rows, LAT8, cols), F32), ((2, LAT8, cols), F32)],
        [SMEM] + [VMEM] * 5 + [ANY] * 2,
        dec_scratch(rows),
        2,
    )(timesteps, enc0, mid0, x_t, w_skip_t, taps, dec_cat, bias)

    bundle = ((chans // 2 + 2 * TILE, cols), BF16)
    mid1, to_one, to_two = call(
        mid_first_kernel, [((chans, low), BF16), bundle, bundle], [VMEM] * 7
    )(low0, q0, q0_other, w_tmid_t, w_up_t, base, near)
    got_one, got_two = exchange(to_one, to_two)

    low1, q1 = call(down_last_kernel, down_outs, [VMEM] + [ANY] * 2, down_scratch, 2)(enc1, w_down_t, bias)
    q1_other = swap(q1)

    (mid2,) = call(mid_last_kernel, [((rows, chans, cols), BF16)], [VMEM] * 5)(low1, q1, q1_other, w_tmid_t, w_up_t)

    enc2, x1 = call(
        enc_last_kernel,
        [((rows, chans, cols), BF16), ((rows, LAT8, cols), F32)],
        [VMEM] * 5 + [ANY] * 2,
        enc_scratch(rows),
        2,
    )(base, near, got_one, got_two, taps, enc_cat, bias)

    feat_other = swap(jnp.where(first, mid2, enc2))

    (x2,) = call(
        dec_last_kernel,
        [((rows, LAT8, cols), F32)],
        [SMEM] + [VMEM] * 7 + [ANY] * 2,
        [((chans, (rows // 2 + 2) * cols), BF16)] + dec_scratch(rows + 2),
        2,
    )(timesteps, enc1, mid1, got_one, got_two, x1, w_skip_t, taps, dec_cat, bias)

    flat = x2[:, :lat].transpose(0, 2, 1).reshape(rows, cols * lat)
    halves = jnp.stack([flat[:, : cols * lat // 2], flat[:, cols * lat // 2 :]])
    x_keep, x_far = mine(halves), swap(theirs(halves))
    result = jnp.where(first, jnp.stack([x_keep, x_far]), jnp.stack([x_far, x_keep]))
    features = jnp.where(first, jnp.stack([enc2, feat_other]), jnp.stack([feat_other, mid2]))
    return (result, features.transpose(0, 1, 3, 2)[None])


def solution(mesh):
    placed = (
        P("clips", "rows", "segment"),
        P("segment", "clips", "rows", None, None),
        P("clips"),
    ) + (P(),) * 9
    return jax.shard_map(
        step_pair,
        mesh=mesh,
        in_specs=placed,
        out_specs=(P("clips", "rows", "segment"), P("segment", "clips", "rows", None, None)),
        check_vma=False,
    )
```

```python
import math

import jax
import jax.numpy as jnp
from jax import lax
from jax.experimental import pallas as pl
from jax.experimental.pallas import tpu as pltpu
from jax.sharding import PartitionSpec as P


EPSILON = 1e-06
LAT8 = 8
TILE = 16
F32 = jnp.float32
BF16 = jnp.bfloat16

VMEM = pl.BlockSpec(memory_space=pltpu.VMEM)
SMEM = pl.BlockSpec(memory_space=pltpu.SMEM)
ANY = pl.BlockSpec(memory_space=pl.ANY)


def act(values):
    scale = lax.rsqrt(jnp.mean(values * values, axis=0, keepdims=True) + EPSILON)
    half = values * (0.5 * scale)
    return half + half * jnp.tanh(half)


def dot(left, right):
    return jnp.dot(left, right, preferred_element_type=F32)


def shifted(values, by):
    count = values.shape[1]
    column = lax.broadcasted_iota(jnp.int32, values.shape, 1)
    edge = 0 if by == 1 else count - 1
    return jnp.where(column == edge, 0.0, pltpu.roll(values, by % count, 1))


def call(kernel, outs, in_specs, scratch=(), copies=0, out_specs=None):
    shapes = [pltpu.VMEM(s, d) for s, d in scratch]
    if copies:
        shapes.append(pltpu.SemaphoreType.DMA((copies,)))
    return pl.pallas_call(
        kernel,
        out_shape=[jax.ShapeDtypeStruct(s, d) for s, d in outs],
        in_specs=in_specs,
        out_specs=out_specs or [VMEM] * len(outs),
        scratch_shapes=shapes,
    )


def edges_of():
    place = lax.axis_index("rows")
    return (place == 0, place == lax.axis_size("rows") - 1)


def coefficient(times_ref, step):
    stamp = jnp.full((LAT8, 128), times_ref[step], jnp.int32)
    return (stamp.astype(F32) + 1.0) / 1000.0


def one_hot_sum(values, hot):
    high = values.astype(BF16)
    rest = values - high.astype(F32)
    middle = rest.astype(BF16)
    low = (rest - middle.astype(F32)).astype(BF16)
    return (dot(high, hot) + dot(middle, hot)) + dot(low, hot)


def one_hot(shape, matches):
    rows = lax.broadcasted_iota(jnp.int32, shape, 0)
    lanes = lax.broadcasted_iota(jnp.int32, shape, 1)
    return jnp.where(matches(rows, lanes), 1.0, 0.0).astype(BF16)


def split_latent(values, cols, exact):
    lat = values.shape[1] // cols
    lane = lax.broadcasted_iota(jnp.int32, (LAT8, values.shape[1]), 1)
    chan = lax.broadcasted_iota(jnp.int32, (LAT8, values.shape[1]), 0)
    wide = jnp.concatenate(
        [jnp.where(lane % lat == chan, values[row : row + 1], 0.0) for row in range(values.shape[0])], axis=0
    )
    hot = one_hot((values.shape[1], cols), lambda r, c: r // lat == c)
    split = one_hot_sum(wide, hot) if exact else dot(wide.astype(BF16), hot)
    return [split[row * LAT8 : (row + 1) * LAT8] for row in range(values.shape[0])]


def join_latent(pieces, lat):
    cols = pieces[0].shape[1]
    hot = one_hot((cols, cols * lat), lambda r, c: c // lat == r)
    wide = one_hot_sum(jnp.concatenate(pieces, axis=0), hot)
    lane = lax.broadcasted_iota(jnp.int32, wide.shape, 1)
    chan = lax.broadcasted_iota(jnp.int32, wide.shape, 0) % LAT8
    wide = jnp.where(lane % lat == chan, wide, 0.0)
    return [
        jnp.sum(wide[row * LAT8 : (row + 1) * LAT8], axis=0, keepdims=True) for row in range(len(pieces))
    ]


def whole_columns(first, near, far):
    return jnp.concatenate([jnp.where(first, near, far), jnp.where(first, far, near)], axis=1)


def spread_bias(bias_ref, step):
    bias_ref[...] = jnp.broadcast_to(bias_ref[:, step : step + 1], bias_ref.shape)


def edges_kernel(latent_ref, stale_hbm, one_hbm, two_hbm, state_hbm, latent_out, part_ref, sems):
    segment = lax.axis_index("segment")
    even = lax.axis_index("rows") % 2 == 0
    rows, _, width = latent_ref.shape
    chans, cols = stale_hbm.shape[3:]
    pieces = width // cols
    halo = 3
    index_one = jnp.where(even, rows - 1, 0)
    index_two = jnp.where(even, 0, rows - 1)
    pairs = [(stale_hbm.at[0, 1 - segment], state_hbm)]
    for slot, frame in enumerate((segment, 1 - segment)):
        pairs.append((stale_hbm.at[0, frame, index_one], one_hbm.at[slot, pl.ds(0, chans)]))
        pairs.append((stale_hbm.at[0, frame, index_two], two_hbm.at[slot, pl.ds(0, chans)]))
    copies = fetches(pairs, sems)
    first = segment == 0
    frames = [jnp.where(first, latent_ref[:, k, :], latent_ref[:, 1 - k, :]) for k in range(2)]
    latent_out[...] = frames[1]
    late = []
    for slot in range(2):
        last, top = frames[slot][rows - halo :], frames[slot][:halo]
        for which, piece in enumerate((jnp.where(even, last, top), jnp.where(even, top, last))):
            flat = [piece[:, k * cols : (k + 1) * cols] for k in range(pieces)]
            flat.append(jnp.zeros((TILE - pieces * halo, cols), F32))
            part_ref[which, slot] = jnp.concatenate(flat, axis=0).astype(BF16)
            target = (one_hbm, two_hbm)[which].at[slot, pl.ds(chans, TILE)]
            late.append((part_ref.at[which, slot], target))
    for offset, (src, dst) in enumerate(late):
        copy = pltpu.make_async_copy(src, dst, sems.at[len(pairs) + offset])
        copy.start()
        copies.append(copy)
    for copy in copies:
        copy.wait()


def fetches(pairs, sems):
    copies = [pltpu.make_async_copy(s, d, sems.at[i]) for i, (s, d) in enumerate(pairs)]
    for copy in copies:
        copy.start()
    return copies


def prep_kernel(
    gated_ref, enc_hbm, dec_hbm, down_hbm, time_hbm, enc_out, dec_out, down_out, bias_out,
    enc_ref, dec_ref, down_ref, time_ref, enc_t, dec_t, down_t, bias_t, sems,
):
    pairs = []
    for hbm, ref in ((dec_hbm, dec_ref), (down_hbm, down_ref), (enc_hbm, enc_ref)):
        pairs += [(hbm.at[dy], ref.at[dy]) for dy in range(3)]
    pairs += [(time_hbm, time_ref)]
    copies = fetches(pairs, sems)
    count = len(pairs)
    outs = []

    def send(src, dst):
        copy = pltpu.make_async_copy(src, dst, sems.at[count + len(outs)])
        copy.start()
        outs.append(copy)

    arrived = iter(copies)
    for src, turned, dst in ((dec_ref, dec_t, dec_out), (down_ref, down_t, down_out), (enc_ref, enc_t, enc_out)):
        chans = src.shape[2]
        for dy in range(3):
            next(arrived).wait()
            for dx in range(3):
                lane = (3 * dy + dx) * chans
                turned[:, lane : lane + chans] = src[dy, dx].T
        send(turned, dst)
    next(arrived).wait()
    biases = dot(gated_ref[...], time_ref[...]).T
    bias_t[:, : biases.shape[1]] = biases
    bias_t[:, biases.shape[1] :] = jnp.zeros((bias_t.shape[0], bias_t.shape[1] - biases.shape[1]), F32)
    send(bias_t, bias_out)
    for copy in outs:
        copy.wait()


def turn_kernel(tmid_hbm, out_ref, tmid_ref, sems):
    far = 2 - 2 * lax.axis_index("segment")
    copies = fetches(((tmid_hbm.at[1], tmid_ref.at[0]), (tmid_hbm.at[far], tmid_ref.at[1])), sems)
    for k, copy in enumerate(copies):
        copy.wait()
        out_ref[k] = tmid_ref[k].T


def store_taps(taps_ref, row, value):
    chans, cols = value.shape
    span = slice(row * cols, (row + 1) * cols)
    taps_ref[:chans, span] = shifted(value, 1).astype(BF16)
    taps_ref[chans : 2 * chans, span] = value.astype(BF16)
    taps_ref[2 * chans :, span] = shifted(value, -1).astype(BF16)


def conv_pairs(count, cols, front, back, w_ref, taps_ref, acc_ref, ready):
    front(0)
    front(2)
    ready()
    for pair in range(0, count, 2):
        window = jnp.concatenate(
            [taps_ref[:, (pair + dy) * cols : (pair + dy + 2) * cols] for dy in range(3)], axis=0
        )
        acc_ref[:, pair * cols : (pair + 2) * cols] = dot(w_ref[...], window)
        if pair + 4 <= count:
            front(pair + 4)
        if pair:
            back(pair - 2)
    back(count - 2)


def encode_rows(ext, w_in, w_ref, bias_ref, ready, border, out_ref, lift_ref, taps_ref, acc_ref):
    count, _, cols = out_ref.shape
    is_first, is_last = edges_of()

    def front(row):
        lifted = dot(w_in, jnp.concatenate(ext[row : row + 2], axis=1).astype(BF16))
        lift_ref[:, row * cols : (row + 2) * cols] = lifted
        for k in range(2):
            store_taps(taps_ref, row + k, act(lifted[:, k * cols : (k + 1) * cols]))

    def back(pair):
        for row in (pair, pair + 1):
            here = slice(row * cols, (row + 1) * cols)
            there = slice((row + 1) * cols, (row + 2) * cols)
            total = lift_ref[:, there] + acc_ref[:, here] + bias_ref[...]
            if row < border:
                total = jnp.where(is_first, 0.0, total)
            if row >= count - border:
                total = jnp.where(is_last, 0.0, total)
            out_ref[row] = total.astype(BF16)

    conv_pairs(count, cols, front, back, w_ref, taps_ref, acc_ref, ready)


def turned_w_in(w_small_ref):
    return w_small_ref[9 * LAT8 :, :].astype(F32).T.astype(BF16)


def neighbour(even, one, two, above):
    return jnp.where(even, two, one) if above else jnp.where(even, one, two)


def down_rows(read_row, w_ref, bias_ref, ready, low_ref, q_ref, acat_ref, cols):
    half = cols // 2
    low_rows = low_ref.shape[1] // half
    chans = acat_ref.shape[0] // 9
    source = lax.broadcasted_iota(jnp.int32, (cols, 2 * cols), 0)
    target = lax.broadcasted_iota(jnp.int32, (cols, 2 * cols), 1)
    wanted = 2 * (target % half) + target // cols
    pick = jnp.where(source == wanted, 1.0, 0.0).astype(BF16)
    column = lax.broadcasted_iota(jnp.int32, (chans, cols), 1)
    for row in range(2 * low_rows + 1):
        gate = act(read_row(row).astype(F32)).astype(BF16)
        both = dot(gate, pick)
        even, odd = both[:, :cols], both[:, cols:]
        before = jnp.where(column % half == 0, 0.0, pltpu.roll(odd, 1, 1))
        parts = [part.astype(BF16) for part in (before, even, odd)]
        for dy in range(3):
            if (row - dy) % 2 or not 0 <= (row - dy) // 2 < low_rows:
                continue
            low = (row - dy) // 2
            lane = (low % 2) * half
            for dx, part in enumerate(parts):
                start = (3 * dy + dx) * chans
                acat_ref[start : start + chans, low * half : (low + 1) * half] = part[:, lane : lane + half]
    ready()
    low_ref[...] = dot(w_ref[...], acat_ref[...])
    for low in range(0, low_ref.shape[1], cols):
        wide = min(cols, low_ref.shape[1] - low)
        total = low_ref[:, low : low + wide] + bias_ref[:, :wide]
        low_ref[:, low : low + wide] = total
        q_ref[:, low : low + wide] = act(total).astype(BF16)


def raise_rows(low_ref, q_ref, other_ref, w_tmid_ref, w_up_ref):
    mixed = low_ref[...] + dot(w_tmid_ref[0], q_ref[...]) + dot(w_tmid_ref[1], other_ref[...])
    return dot(w_up_ref[...], mixed.astype(BF16)).astype(BF16)


def doubling(half, rows):
    source = lax.broadcasted_iota(jnp.int32, (rows * half, 2 * rows * half), 0)
    target = lax.broadcasted_iota(jnp.int32, (rows * half, 2 * rows * half), 1)
    return jnp.where(source == target // 2, 1.0, 0.0).astype(BF16)


def mid_first_kernel(
    low_ref, q_ref, other_ref, w_tmid_ref, w_up_ref, base_ref, near_ref, raised_ref, one_ref, two_ref
):
    raised_ref[...] = raise_rows(low_ref, q_ref, other_ref, w_tmid_ref, w_up_ref)
    rows, _, cols = base_ref.shape
    half = cols // 2
    packed = raised_ref.shape[0] // 2
    start = raised_ref.shape[1] - half
    even = lax.axis_index("rows") % 2 == 0

    def bundle(index, lane, edge):
        piece = raised_ref[:, lane : lane + half]
        sent = jnp.concatenate([near_ref[index], base_ref[edge]], axis=0)
        high = sent.astype(BF16)
        low = (sent - high.astype(F32)).astype(BF16)
        folded = jnp.concatenate([piece[:packed], piece[packed:]], axis=1)
        return jnp.concatenate([folded, high, low], axis=0)

    up = bundle(0, 0, 0)
    down = bundle(1, start, rows - 1)
    one_ref[...] = jnp.where(even, down, up)
    two_ref[...] = jnp.where(even, up, down)


def decode_rows(count, cols, read_joined, w_ref, w_skip_ref, bias_ref, ready, border, w_small_ref, mixed_ref, taps_ref, acc_ref):
    is_first, is_last = edges_of()
    span = 3 * LAT8
    parts = []

    def front(row):
        mixed = dot(w_skip_ref[...], jnp.concatenate([read_joined(row), read_joined(row + 1)], axis=1))
        mixed_ref[:, row * cols : (row + 2) * cols] = mixed
        for k in range(2):
            store_taps(taps_ref, row + k, act(mixed[:, k * cols : (k + 1) * cols]))

    def back(pair):
        outs = []
        for row in (pair, pair + 1):
            here = slice(row * cols, (row + 1) * cols)
            there = slice((row + 1) * cols, (row + 2) * cols)
            value = act(mixed_ref[:, there] + acc_ref[:, here] + bias_ref[...])
            if row < border:
                value = jnp.where(is_first, 0.0, value)
            if row >= count - border:
                value = jnp.where(is_last, 0.0, value)
            outs.append(value.astype(BF16))
        taps = dot(w_small_ref[: 9 * LAT8, :], jnp.concatenate(outs, axis=1))
        for k in range(2):
            tap = taps[:, k * cols : (k + 1) * cols]
            parts.append(shifted(tap[:span], 1) + tap[span : 2 * span] + shifted(tap[2 * span :], -1))

    conv_pairs(count, cols, front, back, w_ref, taps_ref, acc_ref, ready)
    return parts


def tap_sum(parts, row):
    total = None
    for dy in range(3):
        source = row + dy - 1
        if 0 <= source < len(parts):
            piece = parts[source][dy * LAT8 : (dy + 1) * LAT8]
            total = piece if total is None else total + piece
    return total


def waiter(copies, bias_ref, step):
    def ready():
        for copy in copies:
            copy.wait()
        spread_bias(bias_ref, step)

    return ready


def first_kernel(
    times_ref, latent_ref, x_got_ref, got_ref, one_ref, two_ref, far_ref, w_skip_ref, w_small_ref,
    stale_hbm, w_dec_hbm, w_down_hbm, bias_hbm,
    base_ref, near_ref, low_ref, q_ref,
    own_ref, enc_ref, mid_ref, w_dec_ref, w_down_ref, b_dec_ref, b_mid_ref, mixed_ref, taps_ref, acc_ref, acat_ref, sems,
):
    rows, chans, cols = got_ref.shape
    mid = low_ref.shape[0]
    total = bias_hbm.shape[0]
    segment = lax.axis_index("segment")
    first = segment == 0
    even = lax.axis_index("rows") % 2 == 0
    copies = fetches(
        (
            (stale_hbm.at[0, segment], own_ref),
            (w_dec_hbm, w_dec_ref),
            (bias_hbm.at[total - chans :], b_dec_ref),
            (w_down_hbm, w_down_ref),
            (bias_hbm.at[chans : chans + mid], b_mid_ref),
        ),
        sems,
    )
    copies[0].wait()
    for row in range(rows + 2):
        if 1 <= row <= rows:
            own, got = own_ref[row - 1], got_ref[row - 1]
        else:
            own = neighbour(even, one_ref[0, :chans], two_ref[0, :chans], row == 0)
            got = neighbour(even, far_ref[0, :chans], far_ref[1, :chans], row == 0)
        enc_ref[row] = jnp.where(first, own, got)
        mid_ref[row] = jnp.where(first, got, own)
    parts = decode_rows(
        rows, cols, lambda row: jnp.concatenate([mid_ref[row], enc_ref[row]], axis=0),
        w_dec_ref, w_skip_ref, b_dec_ref, waiter(copies[1:3], b_dec_ref, 0), 0, w_small_ref,
        mixed_ref, taps_ref, acc_ref,
    )
    mine = jnp.where(first, latent_ref[:, 0, :], latent_ref[:, 1, :])
    x_rows = split_latent(whole_columns(first, mine, x_got_ref[...]), cols, True)
    coef = coefficient(times_ref, 0)
    near_ref[0] = coef * tap_sum(parts, -1)
    near_ref[1] = coef * tap_sum(parts, rows)
    for row in range(rows):
        base_ref[row] = x_rows[row] - coef * tap_sum(parts, row)
    down_rows(
        lambda row: enc_ref[row], w_down_ref, b_mid_ref, waiter(copies[3:], b_mid_ref, 0),
        low_ref, q_ref, acat_ref, cols,
    )


def second_kernel(
    latent_ref, x_got_ref, one_ref, two_ref, far_ref, w_small_ref, w_enc_hbm, w_down_hbm, bias_hbm,
    enc_ref, low_ref, q_ref,
    w_enc_ref, w_down_ref, b_enc_ref, b_mid_ref, lift_ref, taps_ref, acc_ref, acat_ref, sems,
):
    _, chans, cols = enc_ref.shape
    mid = low_ref.shape[0]
    first = lax.axis_index("segment") == 0
    even = lax.axis_index("rows") % 2 == 0
    copies = fetches(
        (
            (w_enc_hbm, w_enc_ref),
            (bias_hbm.at[:chans], b_enc_ref),
            (w_down_hbm, w_down_ref),
            (bias_hbm.at[chans : chans + mid], b_mid_ref),
        ),
        sems,
    )
    halo = 3
    pieces = latent_ref.shape[2] // cols

    def received(block):
        block = block[chans:].astype(F32)
        return jnp.concatenate([block[k * halo : (k + 1) * halo] for k in range(pieces)], axis=1)

    def halo_rows(above):
        near = neighbour(even, received(one_ref[0]), received(two_ref[0]), above)
        far = neighbour(even, received(far_ref[0]), received(far_ref[1]), above)
        return whole_columns(first, near, far)

    mine = jnp.where(first, latent_ref[:, 0, :], latent_ref[:, 1, :])
    values = jnp.concatenate(
        [halo_rows(True), whole_columns(first, mine, x_got_ref[...]), halo_rows(False)], axis=0
    )
    encode_rows(
        split_latent(values, cols, False), turned_w_in(w_small_ref), w_enc_ref, b_enc_ref,
        waiter(copies[:2], b_enc_ref, 0), 2, enc_ref, lift_ref, taps_ref, acc_ref,
    )
    down_rows(
        lambda row: enc_ref[row + 1], w_down_ref, b_mid_ref, waiter(copies[2:], b_mid_ref, 1),
        low_ref, q_ref, acat_ref, cols,
    )


def third_kernel(
    low_ref, q_ref, other_ref, base_ref, near_ref, one_ref, two_ref, w_small_ref, w_up_ref,
    w_enc_hbm, w_tmid_hbm, bias_hbm,
    send_ref, keep_ref, x_ref,
    enc_ref, w_enc_ref, w_tmid_ref, b_enc_ref, lift_ref, taps_ref, acc_ref, sems,
):
    rows, chans, cols = enc_ref.shape
    first = lax.axis_index("segment") == 0
    even = lax.axis_index("rows") % 2 == 0
    is_first, is_last = edges_of()
    copies = fetches(
        ((w_enc_hbm, w_enc_ref), (bias_hbm.at[:chans], b_enc_ref), (w_tmid_hbm, w_tmid_ref)), sems
    )
    packed = one_ref.shape[0] - 2 * TILE

    def received(above):
        high = neighbour(even, one_ref[packed : packed + TILE, :], two_ref[packed : packed + TILE, :], above)
        low = neighbour(even, one_ref[packed + TILE :, :], two_ref[packed + TILE :, :], above)
        both = high.astype(F32) + low.astype(F32)
        return both[:LAT8], both[LAT8:]

    from_up, base_up = received(True)
    from_down, base_down = received(False)
    ext = [base_ref[row] for row in range(rows)]
    ext[0] = ext[0] - from_up
    ext[-1] = ext[-1] - from_down
    for row in range(rows):
        x_ref[row] = ext[row]
    ext = (
        [jnp.where(is_first, 0.0, base_up - near_ref[0])]
        + ext
        + [jnp.where(is_last, 0.0, base_down - near_ref[1])]
    )
    encode_rows(
        ext, turned_w_in(w_small_ref), w_enc_ref, b_enc_ref, waiter(copies[:2], b_enc_ref, 1), 0,
        enc_ref, lift_ref, taps_ref, acc_ref,
    )
    copies[2].wait()
    raised = raise_rows(low_ref, q_ref, other_ref, w_tmid_ref, w_up_ref)
    wide = dot(raised, doubling(cols // 2, rows // 2)).astype(BF16)
    for row in range(rows):
        low = row // 2
        mid = wide[:, low * cols : (low + 1) * cols]
        enc = enc_ref[row]
        send_ref[row] = jnp.where(first, mid, enc)
        keep_ref[row] = jnp.where(first, enc, mid)


def last_kernel(
    times_ref, enc_ref, mid_ref, one_ref, two_ref, x_ref, w_skip_ref, w_small_ref, w_hbm, bias_hbm,
    send_ref, keep_ref, wide_ref, w_ref, bias_ref, mixed_ref, taps_ref, acc_ref, sems,
):
    rows = x_ref.shape[0]
    chans, cols = enc_ref.shape[1:]
    total = bias_hbm.shape[0]
    copies = fetches(((w_hbm, w_ref), (bias_hbm.at[total - chans :], bias_ref)), sems)
    half = cols // 2
    inner = rows // 2
    first = lax.axis_index("segment") == 0
    even = lax.axis_index("rows") % 2 == 0
    packed = chans // 2
    wide_ref[:, cols : (inner + 1) * cols] = dot(mid_ref[...], doubling(half, inner)).astype(BF16)
    twice = doubling(half, 1)
    for low in (0, inner + 1):
        folded = neighbour(even, one_ref[:packed, :], two_ref[:packed, :], low == 0)
        piece = jnp.concatenate([folded[:, :half], folded[:, half:]], axis=0)
        wide_ref[:, low * cols : (low + 1) * cols] = dot(piece, twice).astype(BF16)

    def joined(row):
        low = row // 2
        return jnp.concatenate([wide_ref[:, low * cols : (low + 1) * cols], enc_ref[row]], axis=0)

    parts = decode_rows(
        rows + 2, cols, joined, w_ref, w_skip_ref, bias_ref, waiter(copies, bias_ref, 1), 1, w_small_ref,
        mixed_ref, taps_ref, acc_ref,
    )
    coef = coefficient(times_ref, 1)
    width = send_ref.shape[1]
    pieces = [x_ref[row] - coef * tap_sum(parts, row + 1) for row in range(rows)]
    for row, flat in enumerate(join_latent(pieces, 2 * width // cols)):
        near, far = flat[:, :width], flat[:, width:]
        keep_ref[row : row + 1, :] = jnp.where(first, near, far)
        send_ref[row : row + 1, :] = jnp.where(first, far, near)


def gated_times(timesteps, half):
    freqs = jnp.exp(-math.log(10000.0) * jnp.arange(half).astype(F32) / half)
    angles = timesteps.astype(F32)[:, None] * freqs[None, :]
    embedded = jnp.concatenate([jnp.sin(angles), jnp.cos(angles)], axis=1)
    gated = jax.nn.silu(embedded).astype(BF16)
    return jnp.pad(gated, ((0, TILE - gated.shape[0]), (0, 0)))


def step_pair(latent, stale, timesteps, w_in, w_enc, w_down, w_tmid, w_up, w_skip, w_dec, w_out, w_time):
    first = lax.axis_index("segment") == 0
    size = lax.axis_size("rows")
    chan_major = stale.transpose(0, 1, 2, 4, 3)
    _, frames, rows, chans, cols = chan_major.shape
    row_major = latent.transpose(1, 0, 2)
    mid = w_down.shape[3]
    lat = w_in.shape[0]
    width = latent.shape[2]
    half = cols // 2
    low = (rows // 2) * half
    wide = 3 * chans
    total = w_time.shape[1]
    assert frames == 2 and lax.axis_size("segment") == 2 and 2 * width == cols * lat

    def paired(start):
        return [p for i in range(start, size - 1, 2) for p in ((i, i + 1), (i + 1, i))]

    def swap(value):
        return lax.ppermute(value, "segment", [(0, 1), (1, 0)])

    def exchange(one, two):
        got_one = lax.ppermute(one, "rows", paired(0))
        got_two = lax.ppermute(two, "rows", paired(1))
        return got_one, got_two

    payload = ((2, chans + TILE, cols), BF16)
    to_one, to_two, to_state, to_latent = call(
        edges_kernel,
        [payload, payload, ((rows, chans, cols), BF16), ((rows, width), F32)],
        [VMEM, ANY],
        [((2, 2, TILE, cols), BF16)],
        9,
        [ANY] * 3 + [VMEM],
    )(row_major, chan_major)
    one, two = exchange(to_one, to_two)
    got = swap(to_state)
    x_got = swap(to_latent)
    far = swap(jnp.stack([one[1], two[1]]))

    taps = jnp.pad(w_out.transpose(1, 0, 3, 2), ((0, 0), (0, 0), (0, LAT8 - lat), (0, 0)))
    w_small = jnp.concatenate(
        [taps.reshape(9 * LAT8, chans), jnp.pad(w_in, ((0, LAT8 - lat), (0, 0)))], axis=0
    )
    w_up_t = w_up.T
    w_skip_t = w_skip.T

    turned = [
        ((chans, 3 * wide), BF16),
        ((chans, 3 * wide), BF16),
        ((mid, 3 * wide), BF16),
        ((total, cols), F32),
    ]
    weights = (w_enc, w_dec, w_down, w_time)
    gated = gated_times(timesteps, w_time.shape[0] // 2)
    w_enc_t, w_dec_t, w_down_t, bias = call(
        prep_kernel, turned, [VMEM] + [ANY] * 4, [(w.shape, BF16) for w in weights] + turned, 14, [ANY] * 4
    )(gated, *weights)

    def conv_scratch(count):
        return [
            ((chans, (count + 2) * cols), F32),
            ((wide, (count + 2) * cols), BF16),
            ((chans, count * cols), F32),
        ]

    w_conv = ((chans, 3 * wide), BF16)
    w_wide = ((mid, 3 * wide), BF16)
    b_conv = ((chans, cols), F32)
    b_wide = ((mid, cols), F32)
    acat = ((3 * wide, low), BF16)
    down_outs = [((mid, low), F32), ((mid, low), BF16)]
    ext = ((rows + 2, chans, cols), BF16)

    base, near, low0, q0 = call(
        first_kernel,
        [((rows, LAT8, cols), F32), ((2, LAT8, cols), F32)] + down_outs,
        [SMEM] + [VMEM] * 8 + [ANY] * 4,
        [((rows, chans, cols), BF16), ext, ext, w_conv, w_wide, b_conv, b_wide] + conv_scratch(rows) + [acat],
        5,
    )(timesteps, row_major, x_got, got, one, two, far, w_skip_t, w_small, chan_major, w_dec_t, w_down_t, bias)
    q0_other = swap(q0)

    (w_tmid_t,) = call(turn_kernel, [((2, mid, mid), BF16)], [ANY], [((2, mid, mid), BF16)], 2)(w_tmid)

    bundle = ((chans // 2 + 2 * TILE, cols), BF16)
    mid1, to_one, to_two = call(
        mid_first_kernel, [((chans, low), BF16), bundle, bundle], [VMEM] * 7
    )(low0, q0, q0_other, w_tmid_t, w_up_t, base, near)
    got_one, got_two = exchange(to_one, to_two)

    enc1, low1, q1 = call(
        second_kernel,
        [((rows + 4, chans, cols), BF16)] + down_outs,
        [VMEM] * 6 + [ANY] * 3,
        [w_conv, w_wide, b_conv, b_wide] + conv_scratch(rows + 4) + [acat],
        4,
    )(row_major, x_got, one, two, far, w_small, w_enc_t, w_down_t, bias)
    q1_other = swap(q1)

    feat_send, feat_keep, x1 = call(
        third_kernel,
        [((rows, chans, cols), BF16)] * 2 + [((rows, LAT8, cols), F32)],
        [VMEM] * 9 + [ANY] * 3,
        [((rows, chans, cols), BF16), w_conv, ((2, mid, mid), BF16), b_conv] + conv_scratch(rows),
        3,
    )(low1, q1, q1_other, base, near, got_one, got_two, w_small, w_up_t, w_enc_t, w_tmid_t, bias)
    feat_got = swap(feat_send)

    x_send, x_keep = call(
        last_kernel,
        [((rows, width), F32)] * 2,
        [SMEM] + [VMEM] * 7 + [ANY] * 2,
        [((chans, (rows // 2 + 2) * cols), BF16), w_conv, b_conv] + conv_scratch(rows + 2),
        2,
    )(timesteps, enc1, mid1, got_one, got_two, x1, w_skip_t, w_small, w_dec_t, bias)
    x_far = swap(x_send)

    features = jnp.where(first, jnp.stack([feat_keep, feat_got]), jnp.stack([feat_got, feat_keep]))
    result = jnp.where(first, jnp.stack([x_keep, x_far]), jnp.stack([x_far, x_keep]))
    return (result, features.transpose(0, 1, 3, 2)[None])


def solution(mesh):
    placed = (
        P("clips", "rows", "segment"),
        P("segment", "clips", "rows", None, None),
        P("clips"),
    ) + (P(),) * 9
    return jax.shard_map(
        step_pair,
        mesh=mesh,
        in_specs=placed,
        out_specs=(P("clips", "rows", "segment"), P("segment", "clips", "rows", None, None)),
        check_vma=False,
    )
```

```python
import math

import jax
import jax.numpy as jnp
from jax import lax
from jax.experimental import pallas as pl
from jax.experimental.pallas import tpu as pltpu
from jax.sharding import PartitionSpec as P


EPSILON = 1e-06
LAT8 = 8
TILE = 16
F32 = jnp.float32
BF16 = jnp.bfloat16

VMEM = pl.BlockSpec(memory_space=pltpu.VMEM)
SMEM = pl.BlockSpec(memory_space=pltpu.SMEM)
ANY = pl.BlockSpec(memory_space=pl.ANY)


def act(values):
    scale = lax.rsqrt(jnp.mean(values * values, axis=0, keepdims=True) + EPSILON)
    half = values * (0.5 * scale)
    return half + half * jnp.tanh(half)


def dot(left, right):
    return jnp.dot(left, right, preferred_element_type=F32)


def shifted(values, by):
    count = values.shape[1]
    column = lax.broadcasted_iota(jnp.int32, values.shape, 1)
    edge = 0 if by == 1 else count - 1
    return jnp.where(column == edge, 0.0, pltpu.roll(values, by % count, 1))


def call(kernel, outs, in_specs, scratch=(), copies=0, out_specs=None):
    shapes = [pltpu.VMEM(s, d) for s, d in scratch]
    if copies:
        shapes.append(pltpu.SemaphoreType.DMA((copies,)))
    return pl.pallas_call(
        kernel,
        out_shape=[jax.ShapeDtypeStruct(s, d) for s, d in outs],
        in_specs=in_specs,
        out_specs=out_specs or [VMEM] * len(outs),
        scratch_shapes=shapes,
    )


def edges_of():
    place = lax.axis_index("rows")
    return (place == 0, place == lax.axis_size("rows") - 1)


def coefficient(times_ref, step):
    stamp = jnp.full((LAT8, 128), times_ref[step], jnp.int32)
    return (stamp.astype(F32) + 1.0) / 1000.0


def one_hot_sum(values, hot):
    high = values.astype(BF16)
    rest = values - high.astype(F32)
    middle = rest.astype(BF16)
    low = (rest - middle.astype(F32)).astype(BF16)
    return (dot(high, hot) + dot(middle, hot)) + dot(low, hot)


def one_hot(shape, matches):
    rows = lax.broadcasted_iota(jnp.int32, shape, 0)
    lanes = lax.broadcasted_iota(jnp.int32, shape, 1)
    return jnp.where(matches(rows, lanes), 1.0, 0.0).astype(BF16)


def split_latent(values, cols, exact):
    lat = values.shape[1] // cols
    lane = lax.broadcasted_iota(jnp.int32, (LAT8, values.shape[1]), 1)
    chan = lax.broadcasted_iota(jnp.int32, (LAT8, values.shape[1]), 0)
    wide = jnp.concatenate(
        [jnp.where(lane % lat == chan, values[row : row + 1], 0.0) for row in range(values.shape[0])], axis=0
    )
    hot = one_hot((values.shape[1], cols), lambda r, c: r // lat == c)
    split = one_hot_sum(wide, hot) if exact else dot(wide.astype(BF16), hot)
    return [split[row * LAT8 : (row + 1) * LAT8] for row in range(values.shape[0])]


def join_latent(pieces, lat):
    cols = pieces[0].shape[1]
    hot = one_hot((cols, cols * lat), lambda r, c: c // lat == r)
    wide = one_hot_sum(jnp.concatenate(pieces, axis=0), hot)
    lane = lax.broadcasted_iota(jnp.int32, wide.shape, 1)
    chan = lax.broadcasted_iota(jnp.int32, wide.shape, 0) % LAT8
    wide = jnp.where(lane % lat == chan, wide, 0.0)
    return [
        jnp.sum(wide[row * LAT8 : (row + 1) * LAT8], axis=0, keepdims=True) for row in range(len(pieces))
    ]


def whole_columns(first, near, far):
    return jnp.concatenate([jnp.where(first, near, far), jnp.where(first, far, near)], axis=1)


def spread_bias(bias_ref, step):
    bias_ref[...] = jnp.broadcast_to(bias_ref[:, step : step + 1], bias_ref.shape)


def edges_kernel(latent_ref, stale_hbm, one_ref, two_ref, state_ref, latent_out, sems):
    segment = lax.axis_index("segment")
    even = lax.axis_index("rows") % 2 == 0
    rows, _, width = latent_ref.shape
    chans, cols = stale_hbm.shape[3:]
    pieces = width // cols
    halo = 3
    index_one = jnp.where(even, rows - 1, 0)
    index_two = jnp.where(even, 0, rows - 1)
    pairs = []
    for slot, frame in enumerate((segment, 1 - segment)):
        pairs.append((stale_hbm.at[0, frame, index_one], one_ref.at[slot, pl.ds(0, chans)]))
        pairs.append((stale_hbm.at[0, frame, index_two], two_ref.at[slot, pl.ds(0, chans)]))
    pairs.append((stale_hbm.at[0, 1 - segment], state_ref))
    copies = fetches(pairs, sems)
    first = segment == 0
    frames = [jnp.where(first, latent_ref[:, k, :], latent_ref[:, 1 - k, :]) for k in range(2)]
    latent_out[...] = frames[1]
    for slot in range(2):
        last, top = frames[slot][rows - halo :], frames[slot][:halo]
        for ref, piece in ((one_ref, jnp.where(even, last, top)), (two_ref, jnp.where(even, top, last))):
            flat = [piece[:, k * cols : (k + 1) * cols] for k in range(pieces)]
            flat.append(jnp.zeros((TILE - pieces * halo, cols), F32))
            ref[slot, chans:] = jnp.concatenate(flat, axis=0).astype(BF16)
    for copy in copies:
        copy.wait()


def fetches(pairs, sems):
    copies = [pltpu.make_async_copy(s, d, sems.at[i]) for i, (s, d) in enumerate(pairs)]
    for copy in copies:
        copy.start()
    return copies


def prep_kernel(
    gated_ref, enc_hbm, dec_hbm, down_hbm, time_hbm, enc_out, dec_out, down_out, bias_out,
    enc_ref, dec_ref, down_ref, time_ref, enc_t, dec_t, down_t, bias_t, sems,
):
    pairs = []
    for hbm, ref in ((dec_hbm, dec_ref), (down_hbm, down_ref), (enc_hbm, enc_ref)):
        pairs += [(hbm.at[dy], ref.at[dy]) for dy in range(3)]
    pairs += [(time_hbm, time_ref)]
    copies = fetches(pairs, sems)
    count = len(pairs)
    outs = []

    def send(src, dst):
        copy = pltpu.make_async_copy(src, dst, sems.at[count + len(outs)])
        copy.start()
        outs.append(copy)

    arrived = iter(copies)
    for src, turned, dst in ((dec_ref, dec_t, dec_out), (down_ref, down_t, down_out), (enc_ref, enc_t, enc_out)):
        chans = src.shape[2]
        for dy in range(3):
            next(arrived).wait()
            for dx in range(3):
                lane = (3 * dy + dx) * chans
                turned[:, lane : lane + chans] = src[dy, dx].T
        send(turned, dst)
    next(arrived).wait()
    biases = dot(gated_ref[...], time_ref[...]).T
    bias_t[:, : biases.shape[1]] = biases
    bias_t[:, biases.shape[1] :] = jnp.zeros((bias_t.shape[0], bias_t.shape[1] - biases.shape[1]), F32)
    send(bias_t, bias_out)
    for copy in outs:
        copy.wait()


def turn_kernel(tmid_hbm, out_ref, tmid_ref, sems):
    far = 2 - 2 * lax.axis_index("segment")
    copies = fetches(((tmid_hbm.at[1], tmid_ref.at[0]), (tmid_hbm.at[far], tmid_ref.at[1])), sems)
    for k, copy in enumerate(copies):
        copy.wait()
        out_ref[k] = tmid_ref[k].T


def store_taps(taps_ref, row, value):
    chans, cols = value.shape
    span = slice(row * cols, (row + 1) * cols)
    taps_ref[:chans, span] = shifted(value, 1).astype(BF16)
    taps_ref[chans : 2 * chans, span] = value.astype(BF16)
    taps_ref[2 * chans :, span] = shifted(value, -1).astype(BF16)


def conv_pairs(count, cols, front, back, w_ref, taps_ref, acc_ref, ready):
    front(0)
    front(2)
    ready()
    for pair in range(0, count, 2):
        window = jnp.concatenate(
            [taps_ref[:, (pair + dy) * cols : (pair + dy + 2) * cols] for dy in range(3)], axis=0
        )
        acc_ref[:, pair * cols : (pair + 2) * cols] = dot(w_ref[...], window)
        if pair + 4 <= count:
            front(pair + 4)
        if pair:
            back(pair - 2)
    back(count - 2)


def encode_rows(ext, w_in, w_ref, bias_ref, ready, border, out_ref, lift_ref, taps_ref, acc_ref):
    count, _, cols = out_ref.shape
    is_first, is_last = edges_of()

    def front(row):
        lifted = dot(w_in, jnp.concatenate(ext[row : row + 2], axis=1).astype(BF16))
        lift_ref[:, row * cols : (row + 2) * cols] = lifted
        for k in range(2):
            store_taps(taps_ref, row + k, act(lifted[:, k * cols : (k + 1) * cols]))

    def back(pair):
        for row in (pair, pair + 1):
            here = slice(row * cols, (row + 1) * cols)
            there = slice((row + 1) * cols, (row + 2) * cols)
            total = lift_ref[:, there] + acc_ref[:, here] + bias_ref[...]
            if row < border:
                total = jnp.where(is_first, 0.0, total)
            if row >= count - border:
                total = jnp.where(is_last, 0.0, total)
            out_ref[row] = total.astype(BF16)

    conv_pairs(count, cols, front, back, w_ref, taps_ref, acc_ref, ready)


def turned_w_in(w_small_ref):
    return w_small_ref[9 * LAT8 :, :].astype(F32).T.astype(BF16)


def neighbour(even, one, two, above):
    return jnp.where(even, two, one) if above else jnp.where(even, one, two)


def down_rows(read_row, w_ref, bias_ref, ready, low_ref, q_ref, acat_ref, cols):
    half = cols // 2
    low_rows = low_ref.shape[1] // half
    chans = acat_ref.shape[0] // 9
    source = lax.broadcasted_iota(jnp.int32, (cols, 2 * cols), 0)
    target = lax.broadcasted_iota(jnp.int32, (cols, 2 * cols), 1)
    wanted = 2 * (target % half) + target // cols
    pick = jnp.where(source == wanted, 1.0, 0.0).astype(BF16)
    column = lax.broadcasted_iota(jnp.int32, (chans, cols), 1)
    for row in range(2 * low_rows + 1):
        gate = act(read_row(row).astype(F32)).astype(BF16)
        both = dot(gate, pick)
        even, odd = both[:, :cols], both[:, cols:]
        before = jnp.where(column % half == 0, 0.0, pltpu.roll(odd, 1, 1))
        parts = [part.astype(BF16) for part in (before, even, odd)]
        for dy in range(3):
            if (row - dy) % 2 or not 0 <= (row - dy) // 2 < low_rows:
                continue
            low = (row - dy) // 2
            lane = (low % 2) * half
            for dx, part in enumerate(parts):
                start = (3 * dy + dx) * chans
                acat_ref[start : start + chans, low * half : (low + 1) * half] = part[:, lane : lane + half]
    ready()
    low_ref[...] = dot(w_ref[...], acat_ref[...])
    for low in range(0, low_ref.shape[1], cols):
        wide = min(cols, low_ref.shape[1] - low)
        total = low_ref[:, low : low + wide] + bias_ref[:, :wide]
        low_ref[:, low : low + wide] = total
        q_ref[:, low : low + wide] = act(total).astype(BF16)


def raise_rows(low_ref, q_ref, other_ref, w_tmid_ref, w_up_ref):
    mixed = low_ref[...] + dot(w_tmid_ref[0], q_ref[...]) + dot(w_tmid_ref[1], other_ref[...])
    return dot(w_up_ref[...], mixed.astype(BF16)).astype(BF16)


def doubling(half, rows):
    source = lax.broadcasted_iota(jnp.int32, (rows * half, 2 * rows * half), 0)
    target = lax.broadcasted_iota(jnp.int32, (rows * half, 2 * rows * half), 1)
    return jnp.where(source == target // 2, 1.0, 0.0).astype(BF16)


def mid_first_kernel(
    low_ref, q_ref, other_ref, w_tmid_ref, w_up_ref, base_ref, near_ref, raised_ref, one_ref, two_ref
):
    raised_ref[...] = raise_rows(low_ref, q_ref, other_ref, w_tmid_ref, w_up_ref)
    rows, _, cols = base_ref.shape
    half = cols // 2
    packed = raised_ref.shape[0] // 2
    start = raised_ref.shape[1] - half
    even = lax.axis_index("rows") % 2 == 0

    def bundle(index, lane, edge):
        piece = raised_ref[:, lane : lane + half]
        sent = jnp.concatenate([near_ref[index], base_ref[edge]], axis=0)
        high = sent.astype(BF16)
        low = (sent - high.astype(F32)).astype(BF16)
        folded = jnp.concatenate([piece[:packed], piece[packed:]], axis=1)
        return jnp.concatenate([folded, high, low], axis=0)

    up = bundle(0, 0, 0)
    down = bundle(1, start, rows - 1)
    one_ref[...] = jnp.where(even, down, up)
    two_ref[...] = jnp.where(even, up, down)


def decode_rows(count, cols, read_joined, w_ref, w_skip_ref, bias_ref, ready, border, w_small_ref, mixed_ref, taps_ref, acc_ref):
    is_first, is_last = edges_of()
    span = 3 * LAT8
    parts = []

    def front(row):
        mixed = dot(w_skip_ref[...], jnp.concatenate([read_joined(row), read_joined(row + 1)], axis=1))
        mixed_ref[:, row * cols : (row + 2) * cols] = mixed
        for k in range(2):
            store_taps(taps_ref, row + k, act(mixed[:, k * cols : (k + 1) * cols]))

    def back(pair):
        outs = []
        for row in (pair, pair + 1):
            here = slice(row * cols, (row + 1) * cols)
            there = slice((row + 1) * cols, (row + 2) * cols)
            value = act(mixed_ref[:, there] + acc_ref[:, here] + bias_ref[...])
            if row < border:
                value = jnp.where(is_first, 0.0, value)
            if row >= count - border:
                value = jnp.where(is_last, 0.0, value)
            outs.append(value.astype(BF16))
        taps = dot(w_small_ref[: 9 * LAT8, :], jnp.concatenate(outs, axis=1))
        for k in range(2):
            tap = taps[:, k * cols : (k + 1) * cols]
            parts.append(shifted(tap[:span], 1) + tap[span : 2 * span] + shifted(tap[2 * span :], -1))

    conv_pairs(count, cols, front, back, w_ref, taps_ref, acc_ref, ready)
    return parts


def tap_sum(parts, row):
    total = None
    for dy in range(3):
        source = row + dy - 1
        if 0 <= source < len(parts):
            piece = parts[source][dy * LAT8 : (dy + 1) * LAT8]
            total = piece if total is None else total + piece
    return total


def waiter(copies, bias_ref, step):
    def ready():
        for copy in copies:
            copy.wait()
        spread_bias(bias_ref, step)

    return ready


def first_kernel(
    times_ref, latent_ref, x_got_ref, got_ref, one_ref, two_ref, far_ref, w_skip_ref, w_small_ref,
    stale_hbm, w_dec_hbm, w_down_hbm, bias_hbm,
    base_ref, near_ref, low_ref, q_ref,
    own_ref, enc_ref, mid_ref, w_dec_ref, w_down_ref, b_dec_ref, b_mid_ref, mixed_ref, taps_ref, acc_ref, acat_ref, sems,
):
    rows, chans, cols = got_ref.shape
    mid = low_ref.shape[0]
    total = bias_hbm.shape[0]
    segment = lax.axis_index("segment")
    first = segment == 0
    even = lax.axis_index("rows") % 2 == 0
    copies = fetches(
        (
            (stale_hbm.at[0, segment], own_ref),
            (w_dec_hbm, w_dec_ref),
            (bias_hbm.at[total - chans :], b_dec_ref),
            (w_down_hbm, w_down_ref),
            (bias_hbm.at[chans : chans + mid], b_mid_ref),
        ),
        sems,
    )
    copies[0].wait()
    for row in range(rows + 2):
        if 1 <= row <= rows:
            own, got = own_ref[row - 1], got_ref[row - 1]
        else:
            own = neighbour(even, one_ref[0, :chans], two_ref[0, :chans], row == 0)
            got = neighbour(even, far_ref[0, :chans], far_ref[1, :chans], row == 0)
        enc_ref[row] = jnp.where(first, own, got)
        mid_ref[row] = jnp.where(first, got, own)
    parts = decode_rows(
        rows, cols, lambda row: jnp.concatenate([mid_ref[row], enc_ref[row]], axis=0),
        w_dec_ref, w_skip_ref, b_dec_ref, waiter(copies[1:3], b_dec_ref, 0), 0, w_small_ref,
        mixed_ref, taps_ref, acc_ref,
    )
    mine = jnp.where(first, latent_ref[:, 0, :], latent_ref[:, 1, :])
    x_rows = split_latent(whole_columns(first, mine, x_got_ref[...]), cols, True)
    coef = coefficient(times_ref, 0)
    near_ref[0] = coef * tap_sum(parts, -1)
    near_ref[1] = coef * tap_sum(parts, rows)
    for row in range(rows):
        base_ref[row] = x_rows[row] - coef * tap_sum(parts, row)
    down_rows(
        lambda row: enc_ref[row], w_down_ref, b_mid_ref, waiter(copies[3:], b_mid_ref, 0),
        low_ref, q_ref, acat_ref, cols,
    )


def second_kernel(
    latent_ref, x_got_ref, one_ref, two_ref, far_ref, w_small_ref, w_enc_hbm, w_down_hbm, bias_hbm,
    enc_ref, low_ref, q_ref,
    w_enc_ref, w_down_ref, b_enc_ref, b_mid_ref, lift_ref, taps_ref, acc_ref, acat_ref, sems,
):
    _, chans, cols = enc_ref.shape
    mid = low_ref.shape[0]
    first = lax.axis_index("segment") == 0
    even = lax.axis_index("rows") % 2 == 0
    copies = fetches(
        (
            (w_enc_hbm, w_enc_ref),
            (bias_hbm.at[:chans], b_enc_ref),
            (w_down_hbm, w_down_ref),
            (bias_hbm.at[chans : chans + mid], b_mid_ref),
        ),
        sems,
    )
    halo = 3
    pieces = latent_ref.shape[2] // cols

    def received(block):
        block = block[chans:].astype(F32)
        return jnp.concatenate([block[k * halo : (k + 1) * halo] for k in range(pieces)], axis=1)

    def halo_rows(above):
        near = neighbour(even, received(one_ref[0]), received(two_ref[0]), above)
        far = neighbour(even, received(far_ref[0]), received(far_ref[1]), above)
        return whole_columns(first, near, far)

    mine = jnp.where(first, latent_ref[:, 0, :], latent_ref[:, 1, :])
    values = jnp.concatenate(
        [halo_rows(True), whole_columns(first, mine, x_got_ref[...]), halo_rows(False)], axis=0
    )
    encode_rows(
        split_latent(values, cols, False), turned_w_in(w_small_ref), w_enc_ref, b_enc_ref,
        waiter(copies[:2], b_enc_ref, 0), 2, enc_ref, lift_ref, taps_ref, acc_ref,
    )
    down_rows(
        lambda row: enc_ref[row + 1], w_down_ref, b_mid_ref, waiter(copies[2:], b_mid_ref, 1),
        low_ref, q_ref, acat_ref, cols,
    )


def third_kernel(
    low_ref, q_ref, other_ref, base_ref, near_ref, one_ref, two_ref, w_small_ref, w_up_ref,
    w_enc_hbm, w_tmid_hbm, bias_hbm,
    send_ref, keep_ref, x_ref,
    enc_ref, w_enc_ref, w_tmid_ref, b_enc_ref, lift_ref, taps_ref, acc_ref, sems,
):
    rows, chans, cols = enc_ref.shape
    first = lax.axis_index("segment") == 0
    even = lax.axis_index("rows") % 2 == 0
    is_first, is_last = edges_of()
    copies = fetches(
        ((w_enc_hbm, w_enc_ref), (bias_hbm.at[:chans], b_enc_ref), (w_tmid_hbm, w_tmid_ref)), sems
    )
    packed = one_ref.shape[0] - 2 * TILE

    def received(above):
        high = neighbour(even, one_ref[packed : packed + TILE, :], two_ref[packed : packed + TILE, :], above)
        low = neighbour(even, one_ref[packed + TILE :, :], two_ref[packed + TILE :, :], above)
        both = high.astype(F32) + low.astype(F32)
        return both[:LAT8], both[LAT8:]

    from_up, base_up = received(True)
    from_down, base_down = received(False)
    ext = [base_ref[row] for row in range(rows)]
    ext[0] = ext[0] - from_up
    ext[-1] = ext[-1] - from_down
    for row in range(rows):
        x_ref[row] = ext[row]
    ext = (
        [jnp.where(is_first, 0.0, base_up - near_ref[0])]
        + ext
        + [jnp.where(is_last, 0.0, base_down - near_ref[1])]
    )
    encode_rows(
        ext, turned_w_in(w_small_ref), w_enc_ref, b_enc_ref, waiter(copies[:2], b_enc_ref, 1), 0,
        enc_ref, lift_ref, taps_ref, acc_ref,
    )
    copies[2].wait()
    raised = raise_rows(low_ref, q_ref, other_ref, w_tmid_ref, w_up_ref)
    wide = dot(raised, doubling(cols // 2, rows // 2)).astype(BF16)
    for row in range(rows):
        low = row // 2
        mid = wide[:, low * cols : (low + 1) * cols]
        enc = enc_ref[row]
        send_ref[row] = jnp.where(first, mid, enc)
        keep_ref[row] = jnp.where(first, enc, mid)


def last_kernel(
    times_ref, enc_ref, mid_ref, one_ref, two_ref, x_ref, w_skip_ref, w_small_ref, w_hbm, bias_hbm,
    send_ref, keep_ref, wide_ref, w_ref, bias_ref, mixed_ref, taps_ref, acc_ref, sems,
):
    rows = x_ref.shape[0]
    chans, cols = enc_ref.shape[1:]
    total = bias_hbm.shape[0]
    copies = fetches(((w_hbm, w_ref), (bias_hbm.at[total - chans :], bias_ref)), sems)
    half = cols // 2
    inner = rows // 2
    first = lax.axis_index("segment") == 0
    even = lax.axis_index("rows") % 2 == 0
    packed = chans // 2
    wide_ref[:, cols : (inner + 1) * cols] = dot(mid_ref[...], doubling(half, inner)).astype(BF16)
    twice = doubling(half, 1)
    for low in (0, inner + 1):
        folded = neighbour(even, one_ref[:packed, :], two_ref[:packed, :], low == 0)
        piece = jnp.concatenate([folded[:, :half], folded[:, half:]], axis=0)
        wide_ref[:, low * cols : (low + 1) * cols] = dot(piece, twice).astype(BF16)

    def joined(row):
        low = row // 2
        return jnp.concatenate([wide_ref[:, low * cols : (low + 1) * cols], enc_ref[row]], axis=0)

    parts = decode_rows(
        rows + 2, cols, joined, w_ref, w_skip_ref, bias_ref, waiter(copies, bias_ref, 1), 1, w_small_ref,
        mixed_ref, taps_ref, acc_ref,
    )
    coef = coefficient(times_ref, 1)
    width = send_ref.shape[1]
    pieces = [x_ref[row] - coef * tap_sum(parts, row + 1) for row in range(rows)]
    for row, flat in enumerate(join_latent(pieces, 2 * width // cols)):
        near, far = flat[:, :width], flat[:, width:]
        keep_ref[row : row + 1, :] = jnp.where(first, near, far)
        send_ref[row : row + 1, :] = jnp.where(first, far, near)


def gated_times(timesteps, half):
    freqs = jnp.exp(-math.log(10000.0) * jnp.arange(half).astype(F32) / half)
    angles = timesteps.astype(F32)[:, None] * freqs[None, :]
    embedded = jnp.concatenate([jnp.sin(angles), jnp.cos(angles)], axis=1)
    gated = jax.nn.silu(embedded).astype(BF16)
    return jnp.pad(gated, ((0, TILE - gated.shape[0]), (0, 0)))


def step_pair(latent, stale, timesteps, w_in, w_enc, w_down, w_tmid, w_up, w_skip, w_dec, w_out, w_time):
    first = lax.axis_index("segment") == 0
    size = lax.axis_size("rows")
    chan_major = stale.transpose(0, 1, 2, 4, 3)
    _, frames, rows, chans, cols = chan_major.shape
    row_major = latent.transpose(1, 0, 2)
    mid = w_down.shape[3]
    lat = w_in.shape[0]
    width = latent.shape[2]
    half = cols // 2
    low = (rows // 2) * half
    wide = 3 * chans
    total = w_time.shape[1]
    assert frames == 2 and lax.axis_size("segment") == 2 and 2 * width == cols * lat

    def paired(start):
        return [p for i in range(start, size - 1, 2) for p in ((i, i + 1), (i + 1, i))]

    def swap(value):
        return lax.ppermute(value, "segment", [(0, 1), (1, 0)])

    def exchange(one, two):
        got_one = lax.ppermute(one, "rows", paired(0))
        got_two = lax.ppermute(two, "rows", paired(1))
        return got_one, got_two

    payload = ((2, chans + TILE, cols), BF16)
    to_one, to_two, to_state, to_latent = call(
        edges_kernel, [payload, payload, ((rows, chans, cols), BF16), ((rows, width), F32)], [VMEM, ANY], (), 5
    )(row_major, chan_major)
    one, two = exchange(to_one, to_two)
    got = swap(to_state)
    x_got = swap(to_latent)
    far = swap(jnp.stack([one[1], two[1]]))

    taps = jnp.pad(w_out.transpose(1, 0, 3, 2), ((0, 0), (0, 0), (0, LAT8 - lat), (0, 0)))
    w_small = jnp.concatenate(
        [taps.reshape(9 * LAT8, chans), jnp.pad(w_in, ((0, LAT8 - lat), (0, 0)))], axis=0
    )
    w_up_t = w_up.T
    w_skip_t = w_skip.T

    turned = [
        ((chans, 3 * wide), BF16),
        ((chans, 3 * wide), BF16),
        ((mid, 3 * wide), BF16),
        ((total, cols), F32),
    ]
    weights = (w_enc, w_dec, w_down, w_time)
    gated = gated_times(timesteps, w_time.shape[0] // 2)
    w_enc_t, w_dec_t, w_down_t, bias = call(
        prep_kernel, turned, [VMEM] + [ANY] * 4, [(w.shape, BF16) for w in weights] + turned, 14, [ANY] * 4
    )(gated, *weights)

    def conv_scratch(count):
        return [
            ((chans, (count + 2) * cols), F32),
            ((wide, (count + 2) * cols), BF16),
            ((chans, count * cols), F32),
        ]

    w_conv = ((chans, 3 * wide), BF16)
    w_wide = ((mid, 3 * wide), BF16)
    b_conv = ((chans, cols), F32)
    b_wide = ((mid, cols), F32)
    acat = ((3 * wide, low), BF16)
    down_outs = [((mid, low), F32), ((mid, low), BF16)]
    ext = ((rows + 2, chans, cols), BF16)

    base, near, low0, q0 = call(
        first_kernel,
        [((rows, LAT8, cols), F32), ((2, LAT8, cols), F32)] + down_outs,
        [SMEM] + [VMEM] * 8 + [ANY] * 4,
        [((rows, chans, cols), BF16), ext, ext, w_conv, w_wide, b_conv, b_wide] + conv_scratch(rows) + [acat],
        5,
    )(timesteps, row_major, x_got, got, one, two, far, w_skip_t, w_small, chan_major, w_dec_t, w_down_t, bias)
    q0_other = swap(q0)

    (w_tmid_t,) = call(turn_kernel, [((2, mid, mid), BF16)], [ANY], [((2, mid, mid), BF16)], 2)(w_tmid)

    bundle = ((chans // 2 + 2 * TILE, cols), BF16)
    mid1, to_one, to_two = call(
        mid_first_kernel, [((chans, low), BF16), bundle, bundle], [VMEM] * 7
    )(low0, q0, q0_other, w_tmid_t, w_up_t, base, near)
    got_one, got_two = exchange(to_one, to_two)

    enc1, low1, q1 = call(
        second_kernel,
        [((rows + 4, chans, cols), BF16)] + down_outs,
        [VMEM] * 6 + [ANY] * 3,
        [w_conv, w_wide, b_conv, b_wide] + conv_scratch(rows + 4) + [acat],
        4,
    )(row_major, x_got, one, two, far, w_small, w_enc_t, w_down_t, bias)
    q1_other = swap(q1)

    feat_send, feat_keep, x1 = call(
        third_kernel,
        [((rows, chans, cols), BF16)] * 2 + [((rows, LAT8, cols), F32)],
        [VMEM] * 9 + [ANY] * 3,
        [((rows, chans, cols), BF16), w_conv, ((2, mid, mid), BF16), b_conv] + conv_scratch(rows),
        3,
    )(low1, q1, q1_other, base, near, got_one, got_two, w_small, w_up_t, w_enc_t, w_tmid_t, bias)
    feat_got = swap(feat_send)

    last = call(
        last_kernel,
        [((rows, width), F32)] * 2,
        [SMEM] + [VMEM] * 7 + [ANY] * 2,
        [((chans, (rows // 2 + 2) * cols), BF16), w_conv, b_conv] + conv_scratch(rows + 2),
        2,
    )
    x_send, x_keep = last(timesteps, enc1, mid1, got_one, got_two, x1, w_skip_t, w_small, w_dec_t, bias)
    x_far = swap(x_send)

    features = jnp.where(first, jnp.stack([feat_keep, feat_got]), jnp.stack([feat_got, feat_keep]))
    result = jnp.where(first, jnp.stack([x_keep, x_far]), jnp.stack([x_far, x_keep]))
    return (result, features.transpose(0, 1, 3, 2)[None])


def solution(mesh):
    placed = (
        P("clips", "rows", "segment"),
        P("segment", "clips", "rows", None, None),
        P("clips"),
    ) + (P(),) * 9
    return jax.shard_map(
        step_pair,
        mesh=mesh,
        in_specs=placed,
        out_specs=(P("clips", "rows", "segment"), P("segment", "clips", "rows", None, None)),
        check_vma=False,
    )
```
